32 devices in a mesh: space: 8 (over y, x, core), member: 4 (over z).
Axes of the slice: x: 2, y: 2, z: 4, core: 2. Of those that a mesh axis runs over, the one named last changes fastest.
Arguments:
- obs_pert: bfloat16 [80, 16384], P('member', 'space'), may hold values from -6 to 6
- innovation: bfloat16 [16384], P('space'), may hold values from -6 to 6
- obs_prec: bfloat16 [16384], P('space'), may hold values from 1 to 100
- obs_lists: int32 [1536, 256], P('space'), may hold values from 0 to 6143
- loc_weight: bfloat16 [1536, 256], P('space'), may hold values from 0.049804688 to 1
- send_rows: int32 [8, 4, 8], P('space'), may hold values from 0 to 47
- ocean_src: int32 [48, 2], P('space'), may hold values from 0 to 31, as said below
- ocean_frac: float32 [48], P('space'), may hold values from 0 to 1
- ocean_ens: bfloat16 [80, 48, 2048], P(None, 'space', 'member'), may hold values from -6 to 6
Outputs:
- ocean_anal: bfloat16 [80, 48, 2048], P(None, 'space', 'member')
The draws below stay inside these ranges and needn't reach their ends.
Inputs may be any that keep to these rules, and one draw needn't show every extreme that they name: `ocean_src`: the two slots of one ocean block differ.
All inputs are finite; a program needn't handle non-finite values.
Results may differ from the reference program's by a relative error of at most 0.0064.
Values may be sent and summed in bfloat16 or wider, within the bound.
A program may use at most 64 MiB of HBM per device.

```python
import math
import jax
import jax.numpy as jnp
from jax import lax

K = 80
OBS_DEV = 2048
LOBS = 256
ABLK_TILE = 192
ITERS = 12
OB_TILE = 6
GROUP = 48
OCELLS = 2048
NOBS = 16384
ABLK = 1536
OBLK = 48
N_SPACE = 8
N_MEMBER = 4
DEVICES = 32


def draw_ocean_src(key, part):

    def one_tile(tile_key):
        key_perm, key_order = jax.random.split(tile_key)
        shuffled = jax.random.permutation(key_perm, DEVICES)
        order = jax.random.permutation(key_order, 2 * OB_TILE)
        values = shuffled[order % DEVICES]
        return values.reshape(OB_TILE, 2)
    tile_keys = jax.random.split(jax.random.fold_in(key, 7), N_SPACE)
    return jax.vmap(one_tile)(tile_keys).reshape(OB_TILE * N_SPACE, 2).astype(jnp.int32)


def touch_ends(result, stream_key, smallest, largest):
    longest = result.shape.index(max(result.shape))
    spots = []
    for shift in (0, 1):
        where = [jax.random.randint(jax.random.fold_in(stream_key, axis), (), 0, length) for axis, length in enumerate(result.shape)]
        where[longest] = (where[longest] + shift) % result.shape[longest]
        spots.append(tuple(where))
    return result.at[spots[0]].set(smallest).at[spots[1]].set(largest)


def steps_of(stream_key, dims, shards, low, high):
    loudness, own = 1.0, jax.random.fold_in(stream_key, 6)
    for position, blocks in shards:
        draws = jnp.exp(jax.random.uniform(jax.random.fold_in(own, position), (blocks,), jnp.float32, low / len(shards), high / len(shards)))
        loudness = loudness * jnp.repeat(draws, dims[position] // blocks).reshape([-1 if axis == position else 1 for axis in range(len(dims))])
    return loudness


def noise(rng, shape, scale, reach, pieces=(), kind=jnp.bfloat16):
    result = scale * jax.random.normal(rng, shape, jnp.float32)
    if pieces:
        result = result * steps_of(rng, shape, pieces, -0.22, 0.18)
    return jnp.clip(result, -reach, reach).astype(kind)


def setup_inputs(seed: int = 0) -> dict:
    keys = jax.random.split(jax.random.key(seed), 10)
    return {
        "obs_pert": noise(keys[0], (K, NOBS), 1.0, 6.0, ((0, 4), (1, 8))),
        "innovation": noise(keys[1], (NOBS,), 1.0, 6.0, ((0, 8),)),
        "obs_prec": jnp.clip(jnp.exp(math.log(100.0) - 4.6051702 * jax.random.uniform(keys[2], (NOBS,), jnp.float32) ** steps_of(keys[2], (NOBS,), ((0, 8),), -0.2, 0.2)), 1.0, 100.0).astype(jnp.bfloat16),
        "obs_lists": touch_ends(jax.random.randint(keys[3], (ABLK, LOBS), 0, 3 * OBS_DEV), jax.random.fold_in(keys[3], 1), 0, (3 * OBS_DEV) - 1).astype(jnp.int32),
        "loc_weight": jnp.clip(0.049804688 + 0.9501953 * jax.random.uniform(keys[4], (ABLK, LOBS), jnp.float32) ** steps_of(keys[4], (ABLK, LOBS), ((0, 8),), -0.2, 0.2), 0.049804688, 1.0).astype(jnp.bfloat16),
        "send_rows": touch_ends(jax.random.randint(keys[5], (N_SPACE, N_MEMBER, N_SPACE), 0, GROUP), jax.random.fold_in(keys[5], 1), 0, GROUP - 1).astype(jnp.int32),
        "ocean_src": draw_ocean_src(jax.random.fold_in(keys[9], 71), 0),
        "ocean_frac": jnp.clip(1.0 * jax.random.uniform(keys[7], (OBLK,), jnp.float32) ** steps_of(keys[7], (OBLK,), ((0, 8),), -0.2, 0.2), 0.0, 1.0),
        "ocean_ens": noise(keys[8], (K, OBLK, OCELLS), 1.0, 6.0, ((1, 8), (2, 4))),
    }


def transform(local_obs, loc_sel, innov_sel, prec_sel):
    members = local_obs.shape[0]
    obs_f32 = local_obs.astype(jnp.float32)
    obs_weight = loc_sel.astype(jnp.float32) * prec_sel.astype(jnp.float32)
    weighted = obs_f32 * obs_weight[None]
    gram = jnp.einsum('ibl,jbl->bij', weighted, obs_f32, precision=lax.Precision.HIGHEST)
    pulled = jnp.einsum('ibl,bl->bi', weighted, innov_sel.astype(jnp.float32), precision=lax.Precision.HIGHEST)
    identity = jnp.eye(members, dtype=jnp.float32)
    precision_mat = (members - 1.0) * identity + gram
    scale_sum = jnp.trace(precision_mat, axis1=1, axis2=2)
    root_start = precision_mat / scale_sum[:, None, None]
    inverse_start = jnp.broadcast_to(identity, precision_mat.shape)

    def newton(iteration, carry):
        root_iter, inverse_iter = carry
        correction = 1.5 * identity - 0.5 * jnp.einsum('bij,bjk->bik', inverse_iter, root_iter, precision=lax.Precision.HIGHEST)
        root_next = jnp.einsum('bij,bjk->bik', root_iter, correction, precision=lax.Precision.HIGHEST)
        inverse_next = jnp.einsum('bij,bjk->bik', correction, inverse_iter, precision=lax.Precision.HIGHEST)
        return (root_next, inverse_next)
    root_iter, inverse_iter = lax.fori_loop(0, ITERS, newton, (root_start, inverse_start))
    spread = jnp.sqrt((members - 1.0) / scale_sum)[:, None, None] * inverse_iter
    half_way = jnp.einsum('bij,bj->bi', inverse_iter, pulled, precision=lax.Precision.HIGHEST)
    mean_weight = jnp.einsum('bij,bj->bi', inverse_iter, half_way, precision=lax.Precision.HIGHEST) / scale_sum[:, None]
    return (spread + mean_weight[:, :, None]).astype(jnp.bfloat16)

def apply_weights(ensemble, trans_one, trans_two, frac):
    frac_col = frac[:, None, None]
    mixed = ((1.0 - frac_col) * trans_one.astype(jnp.float32) + frac_col * trans_two.astype(jnp.float32)).astype(jnp.bfloat16)
    ens_f32 = ensemble.astype(jnp.float32)
    ens_mean = lax.optimization_barrier(jnp.mean(ens_f32, axis=0))
    deviation = (ens_f32 - ens_mean[None]).astype(jnp.bfloat16)
    product = jnp.einsum('jol,oji->iol', deviation.astype(jnp.float32), mixed.astype(jnp.float32))
    return (ens_mean[None] + product).astype(jnp.bfloat16)

def reference(obs_pert, innovation, obs_prec, obs_lists, loc_weight, send_rows, ocean_src, ocean_frac, ocean_ens):
    group_len = ABLK_TILE // N_MEMBER
    total_obs = obs_pert.shape[1]

    def one_tile(tile_idx):
        sources = lax.dynamic_slice_in_dim(ocean_src, tile_idx * OB_TILE, OB_TILE, 0).reshape(-1)
        member_part = sources // N_SPACE
        space_part = sources % N_SPACE
        local_row = send_rows[space_part, member_part, tile_idx]
        block_ids = (space_part * ABLK_TILE + member_part * group_len + local_row).astype(jnp.int32)
        lists = obs_lists[block_ids]
        offsets = (space_part - 1) * OBS_DEV
        global_idx = ((lists + offsets[:, None]) % total_obs).astype(jnp.int32)
        local_obs = obs_pert[:, global_idx]
        weights = transform(local_obs, loc_weight[block_ids], innovation[global_idx], obs_prec[global_idx])
        weights = weights.reshape(OB_TILE, 2, K, K)
        ensemble = lax.dynamic_slice_in_dim(ocean_ens, tile_idx * OB_TILE, OB_TILE, 1)
        frac = lax.dynamic_slice_in_dim(ocean_frac, tile_idx * OB_TILE, OB_TILE, 0)
        return apply_weights(ensemble, weights[:, 0], weights[:, 1], frac)
    tiles = lax.map(one_tile, jnp.arange(N_SPACE, dtype=jnp.int32))
    return jnp.moveaxis(tiles, 0, 1).reshape(K, OB_TILE * N_SPACE, OCELLS)
```

```python
import functools

import jax
import jax.numpy as jnp
from jax import lax
from jax.experimental import pallas as pl
from jax.experimental.pallas import tpu as pltpu
from jax.sharding import PartitionSpec as P

ITERS = 12
LANES = 128
CHUNK = 512
CORES = 2
ROWS16 = 16
PARTS = 2


def split(value):
    high = value.astype(jnp.bfloat16)
    low = (value - high.astype(jnp.float32)).astype(jnp.bfloat16)
    return high, low


def left_side(value):
    return jnp.concatenate(split(value), axis=1)


def right_side(value):
    pair = left_side(value)
    filler = jnp.zeros((LANES - pair.shape[0], pair.shape[1]), jnp.bfloat16)
    return jnp.concatenate([pair, filler, pair, filler], axis=0)


def halves(product):
    return product[:, :LANES] + product[:, LANES:]


def mm(lhs, rhs):
    return jnp.dot(lhs, rhs, preferred_element_type=jnp.float32)


def xor(value, flip, size):
    result, bit = 0, 1
    while bit < size:
        own = (value // bit) % 2
        result = result + (1 - own if flip & bit else own) * bit
        bit *= 2
    return result


MESH = pl.DeviceIdType.MESH


def remote(src, dst, send_sem, recv_sem, device):
    return pltpu.make_async_remote_copy(
        src_ref=src, dst_ref=dst, send_sem=send_sem, recv_sem=recv_sem,
        device_id=device, device_id_type=MESH,
    )


def letkf_kernel(
    ns, nm, picks,
    send_ref, src_ref, frac_ref, lists_hbm, loc_hbm, pert_ref, prec_ref, innov_ref, out_ref,
    lists_ref, loc_ref, loc_f32, pert_all, prec_all, innov_all, innov_f32, rows_list, rows_loc,
    message, table, chosen, dense, gram, gram_in, root, inverse, pulled, scales, mixed, mixed_in,
    local_sem, z_send, z_recv, core_send, core_recv, extra_send, extra_recv,
    list_send, list_recv, gram_send, gram_recv, mix_send, mix_recv,
):
    s = lax.axis_index("space")
    m = lax.axis_index("member")
    nc = ns // CORES
    core, chip = s % CORES, s // CORES
    sibling = (s + 1 - 2 * core, m)
    members = pert_ref.shape[0] * nm
    tile_obs = pert_ref.shape[1]
    tile_his = tile_obs // LANES
    part = tile_obs // PARTS
    group_len = lists_ref.shape[0] // nm
    lobs = lists_ref.shape[1]
    oblocks = out_ref.shape[0]
    slots = mixed.shape[0]
    z_peers = [xor(m, k, nm) for k in range(1, nm)]
    chips = [xor(chip, k, nc) for k in range(1, nc)]
    s_peers = [lax.rem(s + k, ns) for k in range(1, ns)]

    take_lists = pltpu.make_async_copy(lists_hbm, lists_ref, local_sem.at[0])
    take_loc = pltpu.make_async_copy(loc_hbm, loc_ref, local_sem.at[1])
    take_pert = pltpu.make_async_copy(pert_ref, pert_all.at[core, m], local_sem.at[2])
    take_prec = pltpu.make_async_copy(prec_ref, prec_all.at[core], local_sem.at[3])
    take_innov = pltpu.make_async_copy(innov_ref, innov_all.at[core], local_sem.at[4])
    for copy in (take_lists, take_loc, take_pert, take_prec, take_innov):
        copy.start()

    barrier = pltpu.get_barrier_semaphore()
    for peer in z_peers:
        pl.semaphore_signal(barrier, inc=1, device_id=(s, peer), device_id_type=MESH)
    for peer in s_peers:
        pl.semaphore_signal(barrier, inc=1, device_id=(peer, m), device_id_type=MESH)
    pl.semaphore_wait(barrier, len(z_peers) + len(s_peers))

    def span(h):
        return pl.ds(h * part, part)

    def to_z(peer, h):
        return remote(
            pert_ref.at[:, span(h)], pert_all.at[core, m, :, span(h)],
            z_send.at[peer, h], z_recv.at[m, h], (s, peer),
        )

    def from_z(peer, h):
        return remote(
            pert_ref.at[:, span(h)], pert_all.at[core, peer, :, span(h)],
            z_send.at[m, h], z_recv.at[peer, h], (s, peer),
        )

    def across(owner, h, src):
        return remote(
            src, pert_all.at[core, owner, :, span(h)],
            core_send.at[owner, h], core_recv.at[owner, h], sibling,
        )

    def from_across(owner, h):
        there = pert_all.at[1 - core, owner, :, span(h)]
        return remote(there, there, core_send.at[owner, h], core_recv.at[owner, h], sibling)

    for h in range(PARTS):
        for peer in z_peers:
            to_z(peer, h).start()
    extra_out = [
        remote(prec_ref, prec_all.at[core], extra_send.at[0], extra_recv.at[0], sibling),
        remote(innov_ref, innov_all.at[core], extra_send.at[1], extra_recv.at[1], sibling),
    ]
    extra_in = [
        remote(prec_ref, prec_all.at[1 - core], extra_send.at[0], extra_recv.at[0], sibling),
        remote(innov_ref, innov_all.at[1 - core], extra_send.at[1], extra_recv.at[1], sibling),
    ]
    for copy in extra_out:
        copy.start()
    for h in range(PARTS):
        across(m, h, pert_ref.at[:, span(h)]).start()

    take_lists.wait()
    take_loc.wait()
    loc_f32[...] = loc_ref[...].astype(jnp.float32)
    for parity in range(CORES):
        def pick_rows(t, carry):
            for g in range(nm):
                row = send_ref[g, t * CORES + parity] + g * group_len
                rows_list[parity, pl.ds(t * nm + g, 1), :] = lists_ref[pl.ds(row, 1), :]
                rows_loc[parity, pl.ds(t * nm + g, 1), :] = loc_f32[pl.ds(row, 1), :]
            return carry

        lax.fori_loop(0, nc, pick_rows, 0, unroll=nc <= 4)
        spots = rows_list[parity]
        high = lax.shift_right_logical(spots, 7).astype(jnp.float32)
        low = jnp.bitwise_and(spots, LANES - 1).astype(jnp.float32)
        message[parity, :, 0:lobs] = high.astype(jnp.bfloat16)
        message[parity, :, lobs : 2 * lobs] = low.astype(jnp.bfloat16)
        message[parity, :, 2 * lobs : 3 * lobs] = rows_loc[parity].astype(jnp.bfloat16)
    pick_row = lax.broadcasted_iota(jnp.int32, (table.shape[1], LANES), 0)
    tile_of = jnp.zeros((table.shape[1], LANES), jnp.int32)
    group_of = jnp.zeros((table.shape[1], LANES), jnp.int32)
    for p in range(picks):
        q = m * picks + p
        slot = src_ref[q % 2, q // 2]
        tile_of = jnp.where(pick_row == p, slot % ns, tile_of)
        group_of = jnp.where(pick_row == p, slot // ns, group_of)
    for parity in range(CORES):
        message[parity, :, 3 * lobs : 3 * lobs + LANES] = (
            tile_of.astype(jnp.float32).astype(jnp.bfloat16)
        )
        message[parity, :, 3 * lobs + LANES :] = group_of.astype(jnp.float32).astype(jnp.bfloat16)

    def list_to(peer):
        return remote(
            message.at[peer % CORES], table.at[s], list_send.at[peer], list_recv.at[s], (peer, m)
        )

    def list_from(peer):
        return remote(
            message.at[core], table.at[peer], list_send.at[peer], list_recv.at[peer], (peer, m)
        )

    for peer in s_peers:
        list_to(peer).start()
    table[s] = message[core]
    gram[...] = jnp.zeros_like(gram)
    for peer in s_peers:
        list_from(peer).wait_recv()

    deep = nc * ROWS16
    per_tile = table.shape[1]
    tiles_col, rows_col = [], []
    for t in range(nc):
        cut = table[t * CORES + core, 0:ROWS16, 3 * lobs :].astype(jnp.float32)
        tiles_col.append(cut[:, 0:1])
        rows_col.append(cut[:, LANES : LANES + 1] + float(t * nm))
    tiles_col = jnp.concatenate(tiles_col, axis=0).astype(jnp.int32)
    rows_col = jnp.concatenate(rows_col, axis=0).astype(jnp.int32)
    at_row = lax.broadcasted_iota(jnp.int32, (deep, per_tile), 1) == rows_col

    def select(t):
        hot = jnp.where(jnp.logical_and(at_row, tiles_col == t), 1.0, 0.0).astype(jnp.bfloat16)
        return mm(hot, table[t, :, 0 : 3 * lobs])

    if ns <= 8:
        total = select(0)
        for t in range(1, ns):
            total += select(t)
        chosen[...] = total
    else:
        chosen[...] = jnp.zeros_like(chosen)

        def select_step(t, carry):
            chosen[...] += select(t)
            return carry

        lax.fori_loop(0, ns, select_step, 0)
    shift = (tiles_col - 1) * tile_his - chip * (CORES * tile_his)
    spots = chosen[:, 0:lobs] + shift.astype(jnp.float32)
    around = float(ns * tile_his)
    spots = jnp.where(spots < 0.0, spots + around, spots)
    chosen[:, 0:lobs] = jnp.where(spots >= around, spots - around, spots)

    for copy in (take_prec, take_innov):
        copy.wait()
    for copy in extra_in:
        copy.wait_recv()
    innov_f32[...] = innov_all[...].astype(jnp.float32)
    his = CORES * tile_his
    hi_iota = lax.broadcasted_iota(jnp.int32, (his, lobs), 0).astype(jnp.float32)
    lo_iota = lax.broadcasted_iota(jnp.int32, (LANES, lobs), 0).astype(jnp.float32)
    prec = jnp.concatenate([prec_all[i].astype(jnp.float32) for i in range(CORES)], axis=0)
    contract = (((1,), (1,)), ((), ()))

    def spread(t, carry):
        for p in range(picks):
            row = pl.ds(t * ROWS16 + p, 1)
            high, low = chosen[row, 0:lobs], chosen[row, lobs : 2 * lobs]
            taper = chosen[row, 2 * lobs : 3 * lobs]
            hi_hot = jnp.where(hi_iota == high, taper, 0.0).astype(jnp.bfloat16)
            lo_hot = jnp.where(lo_iota == low, 1.0, 0.0).astype(jnp.bfloat16)
            dense[t * picks + p] = prec * lax.dot_general(
                hi_hot, lo_hot, contract, preferred_element_type=jnp.float32
            )
        return carry

    lax.fori_loop(0, nc, spread, 0)

    per = CHUNK // LANES

    def add_part(tile, h):
        def chunk_step(c, carry):
            first = h * part + c * CHUNK
            where = pl.ds(pl.multiple_of(first, CHUNK), CHUNK)
            wide = jnp.concatenate(
                [pert_all[tile, i, :, where].astype(jnp.float32) for i in range(nm)], axis=0
            )
            line = jnp.concatenate(
                [
                    innov_f32[tile, pl.ds(first // LANES + j, 1), :]
                    for j in range(per)
                ],
                axis=1,
            )
            line = jnp.where(
                lax.broadcasted_iota(jnp.int32, (ROWS16, CHUNK), 0) == 0, line, 0.0
            )
            cells = jnp.concatenate([wide, line], axis=0).astype(jnp.bfloat16)

            def pick_step(t, carry):
                for p in range(picks):
                    b = t * picks + p
                    parts = []
                    for j in range(per):
                        at = pl.ds(tile * tile_his + first // LANES + j, 1)
                        parts.append(wide[:, j * LANES : (j + 1) * LANES] * dense[b, at, :])
                    high, low = split(jnp.concatenate(parts, axis=1))
                    gram[b, :, : cells.shape[0]] += lax.dot_general(
                        high, cells, contract, preferred_element_type=jnp.float32
                    ) + lax.dot_general(low, cells, contract, preferred_element_type=jnp.float32)
                return carry

            lax.fori_loop(0, nc, pick_step, 0, unroll=nc <= 4)
            return carry

        lax.fori_loop(0, part // CHUNK, chunk_step, 0)

    def arrive(h):
        for peer in z_peers:
            from_z(peer, h).wait_recv()
            across(peer, h, pert_all.at[core, peer, :, span(h)]).start()

    def arrive_across(h):
        for i in range(nm):
            from_across(i, h).wait_recv()

    take_pert.wait()
    arrive(0)
    add_part(core, 0)
    for h in range(PARTS):
        if h > 0:
            add_part(core, h)
        if h + 1 < PARTS:
            arrive(h + 1)
        arrive_across(h)
        add_part(1 - core, h)

    def gram_to(peer):
        return remote(
            gram.at[pl.ds(peer * picks, picks)], gram_in.at[chip],
            gram_send.at[peer], gram_recv.at[chip], (peer * CORES + core, m),
        )

    def gram_from(peer):
        return remote(
            gram.at[pl.ds(peer * picks, picks)], gram_in.at[peer],
            gram_send.at[peer], gram_recv.at[peer], (peer * CORES + core, m),
        )

    for peer in reversed(chips):
        gram_to(peer).start()

    rows = lax.broadcasted_iota(jnp.int32, (members, LANES), 0)
    cols = lax.broadcasted_iota(jnp.int32, (members, LANES), 1)
    on_diag = rows == cols
    half3 = jnp.where(on_diag, 1.5, 0.0)

    for peer in chips:
        gram_from(peer).wait_recv()
    for p in range(picks):
        both = gram[chip * picks + p]
        for peer in chips:
            both += gram_in[peer, p]
        pulled[p] = jnp.sum(jnp.where(cols == members, both, 0.0), axis=1, keepdims=True)
        matrix = jnp.where(cols < members, both, 0.0) + jnp.where(on_diag, members - 1.0, 0.0)
        scale = jnp.sum(
            jnp.sum(jnp.where(on_diag, matrix, 0.0), axis=1, keepdims=True), axis=0, keepdims=True
        )
        scales[p] = jnp.broadcast_to(scale, (1, LANES))
        start = matrix / scale
        correction = half3 - 0.5 * start
        root[p] = halves(mm(left_side(start), right_side(correction)))
        inverse[p] = correction

    def newton(step, carry):
        corrections, pairs = [], []
        filler = jnp.zeros((LANES - members, 2 * LANES), jnp.bfloat16)
        for p in range(picks):
            r, z = left_side(root[p]), left_side(inverse[p])
            rhs = jnp.concatenate([r, filler, r, filler], axis=0)
            corrections.append(half3 - 0.5 * halves(mm(z, rhs)))
            pairs.append(jnp.concatenate([r, z], axis=0))
        for p in range(picks):
            both = halves(mm(pairs[p], right_side(corrections[p])))
            root[p] = both[:members]
            inverse[p] = both[members:]
        return carry

    lax.fori_loop(0, ITERS - 1, newton, 0)

    sums = [jnp.zeros((members, LANES), jnp.float32) for _ in range(slots)]
    base = (m * picks) // 2
    for p in range(picks):
        z = inverse[p]
        scale = scales[p]
        half_way = jnp.sum(z * pulled[p], axis=0, keepdims=True)
        mean_weight = jnp.sum(z * half_way, axis=1, keepdims=True) / scale[:, :1]
        trans = jnp.sqrt((members - 1.0) / scale) * z + mean_weight
        trans = trans.astype(jnp.bfloat16).astype(jnp.float32)
        q = m * picks + p
        o = q // 2
        frac = frac_ref[o]
        weight = jnp.where(q % 2 == 0, 1.0 - frac, frac)
        for j in range(max(0, p // 2), min(slots, p // 2 + 2)):
            sums[j] += jnp.where(o - base == j, weight, 0.0) * trans
    for j in range(slots):
        mixed[j] = sums[j].astype(jnp.bfloat16)

    def mix_to(peer):
        return remote(mixed, mixed_in.at[m], mix_send.at[peer], mix_recv.at[m], (s, peer))

    def mix_from(peer):
        return remote(mixed, mixed_in.at[peer], mix_send.at[peer], mix_recv.at[peer], (s, peer))

    for peer in z_peers:
        mix_to(peer).start()
    mixed_in[m] = mixed[...]
    for peer in chips:
        gram_to(peer).wait_send()
    for peer in s_peers:
        list_to(peer).wait_send()
    for copy in extra_out:
        copy.wait_send()
    for h in range(PARTS):
        for peer in z_peers:
            to_z(peer, h).wait_send()
            across(peer, h, pert_all.at[core, peer, :, span(h)]).wait_send()
        across(m, h, pert_ref.at[:, span(h)]).wait_send()
    for peer in z_peers:
        mix_from(peer).wait_recv()
    for o in range(oblocks):
        total = None
        for owner in range(nm):
            j = o - (owner * picks) // 2
            if 0 <= j and o <= (owner * picks + picks - 1) // 2:
                term = mixed_in[owner, j].astype(jnp.float32)
                total = term if total is None else total + term
        out_ref[o] = total.astype(jnp.bfloat16)
    for peer in z_peers:
        mix_to(peer).wait_send()


def mixed_weights(send, src, frac, lists, loc, pert, prec, innov):
    ns, nm = lax.axis_size("space"), lax.axis_size("member")
    shard, tile_obs = pert.shape
    members = shard * nm
    oblocks = src.shape[1]
    nc = ns // CORES
    picks = 2 * oblocks // nm
    assert picks * nm == 2 * oblocks and picks <= ROWS16
    slots = picks // 2 + picks % 2
    his = tile_obs // LANES
    lobs = lists.shape[1]
    vmem = pl.BlockSpec(memory_space=pltpu.VMEM)
    hbm = pl.BlockSpec(memory_space=pl.ANY)
    smem = pl.BlockSpec(memory_space=pltpu.SMEM)
    dma = pltpu.SemaphoreType.DMA
    bf16, f32 = jnp.bfloat16, jnp.float32
    blocks = lambda n, kind: pltpu.VMEM((n, members, LANES), kind)
    wide = 3 * lobs + 2 * LANES
    big = nc * nm * ns * wide * 2 > 4 * 2**20
    return pl.pallas_call(
        functools.partial(letkf_kernel, ns, nm, picks),
        in_specs=[smem, smem, smem, hbm, hbm, hbm, hbm, hbm],
        out_specs=vmem,
        out_shape=jax.ShapeDtypeStruct((oblocks, members, LANES), bf16),
        scratch_shapes=[
            pltpu.VMEM(lists.shape, lists.dtype),
            pltpu.VMEM(loc.shape, loc.dtype),
            pltpu.VMEM(loc.shape, f32),
            pltpu.VMEM((CORES, nm, shard, tile_obs), bf16),
            pltpu.VMEM((CORES, his, LANES), bf16),
            pltpu.VMEM((CORES, his, LANES), bf16),
            pltpu.VMEM((CORES, his, LANES), f32),
            pltpu.VMEM((CORES, nc * nm, lobs), lists.dtype),
            pltpu.VMEM((CORES, nc * nm, lobs), f32),
            pltpu.VMEM((CORES, nc * nm, wide), bf16),
            pltpu.VMEM((ns, nc * nm, wide), bf16),
            pltpu.VMEM((nc * ROWS16, 3 * lobs), f32),
            pltpu.VMEM((nc * picks, CORES * his, LANES), f32),
            blocks(nc * picks, f32),
            pltpu.VMEM((nc, picks, members, LANES), f32),
            blocks(picks, f32),
            blocks(picks, f32),
            pltpu.VMEM((picks, members, 1), f32),
            pltpu.VMEM((picks, 1, LANES), f32),
            blocks(slots, bf16),
            pltpu.VMEM((nm, slots, members, LANES), bf16),
            dma((5,)), dma((nm, PARTS)), dma((nm, PARTS)), dma((nm, PARTS)), dma((nm, PARTS)),
            dma((2,)), dma((2,)), dma((ns,)), dma((ns,)), dma((nc,)), dma((nc,)),
            dma((nm,)), dma((nm,)),
        ],
        compiler_params=pltpu.CompilerParams(
            collective_id=0, has_side_effects=True,
            vmem_limit_bytes=56 * 2**20 if big else None,
        ),
        name="mixed_weights",
    )(send, src, frac, lists, loc, pert, prec, innov)


def apply_weights(ensemble, mixed):
    ens_mean = jnp.mean(ensemble, axis=0, dtype=jnp.float32)
    deviation = (ensemble.astype(jnp.float32) - ens_mean[None]).astype(jnp.bfloat16)
    product = jnp.einsum("jol,oji->iol", deviation, mixed, preferred_element_type=jnp.float32)
    return (ens_mean[None] + product).astype(jnp.bfloat16)


def shards(
    obs_pert,
    innovation,
    obs_prec,
    obs_lists,
    loc_weight,
    send_rows,
    ocean_src,
    ocean_frac,
    ocean_ens,
):
    mixed = mixed_weights(
        send_rows[0], ocean_src.T, ocean_frac, obs_lists, loc_weight, obs_pert,
        obs_prec.reshape(-1, LANES), innovation.reshape(-1, LANES),
    )
    mixed = mixed[:, :, : ocean_ens.shape[0]]
    return apply_weights(ocean_ens, mixed)


def solution(mesh):
    return jax.shard_map(
        shards,
        mesh=mesh,
        in_specs=(
            P("member", "space"),
            P("space"),
            P("space"),
            P("space", None),
            P("space", None),
            P("space", None, None),
            P("space", None),
            P("space"),
            P(None, "space", "member"),
        ),
        out_specs=P(None, "space", "member"),
        check_vma=False,
    )
```

```python
import functools

import jax
import jax.numpy as jnp
from jax import lax
from jax.experimental import pallas as pl
from jax.experimental.pallas import tpu as pltpu
from jax.sharding import PartitionSpec as P

ITERS = 12
LANES = 128
CHUNK = 512
CORES = 2
ROWS16 = 16
PARTS = 4


def split(value):
    high = value.astype(jnp.bfloat16)
    low = (value - high.astype(jnp.float32)).astype(jnp.bfloat16)
    return high, low


def left_side(value):
    return jnp.concatenate(split(value), axis=1)


def right_side(value):
    pair = left_side(value)
    filler = jnp.zeros((LANES - pair.shape[0], pair.shape[1]), jnp.bfloat16)
    return jnp.concatenate([pair, filler, pair, filler], axis=0)


def halves(product):
    return product[:, :LANES] + product[:, LANES:]


def mm(lhs, rhs):
    return jnp.dot(lhs, rhs, preferred_element_type=jnp.float32)


def xor(value, flip, size):
    result, bit = 0, 1
    while bit < size:
        own = (value // bit) % 2
        result = result + (1 - own if flip & bit else own) * bit
        bit *= 2
    return result


MESH = pl.DeviceIdType.MESH


def remote(src, dst, send_sem, recv_sem, device):
    return pltpu.make_async_remote_copy(
        src_ref=src, dst_ref=dst, send_sem=send_sem, recv_sem=recv_sem,
        device_id=device, device_id_type=MESH,
    )


def letkf_kernel(
    ns, nm, picks,
    send_ref, src_ref, frac_ref, lists_hbm, loc_hbm, pert_ref, prec_ref, innov_ref, out_ref,
    lists_ref, loc_ref, loc_f32, pert_all, prec_all, innov_all, innov_f32, rows_list, rows_loc,
    message, table, chosen, dense, gram, gram_out, gram_in, root, inverse, pulled, scales, mixed, mixed_in,
    local_sem, z_send, z_recv, core_send, core_recv, extra_send, extra_recv,
    list_send, list_recv, gram_send, gram_recv, mix_send, mix_recv,
):
    s = lax.axis_index("space")
    m = lax.axis_index("member")
    nc = ns // CORES
    core, chip = s % CORES, s // CORES
    sibling = (s + 1 - 2 * core, m)
    members = pert_ref.shape[0] * nm
    tile_obs = pert_ref.shape[1]
    tile_his = tile_obs // LANES
    part = tile_obs // PARTS
    group_len = lists_ref.shape[0] // nm
    lobs = lists_ref.shape[1]
    oblocks = out_ref.shape[0]
    slots = mixed.shape[0]
    z_peers = [xor(m, k, nm) for k in range(1, nm)]
    chips = [xor(chip, k, nc) for k in range(1, nc)]
    s_peers = [lax.rem(s + k, ns) for k in range(1, ns)]

    take_lists = pltpu.make_async_copy(lists_hbm, lists_ref, local_sem.at[0])
    take_loc = pltpu.make_async_copy(loc_hbm, loc_ref, local_sem.at[1])
    take_pert = pltpu.make_async_copy(pert_ref, pert_all.at[core, m], local_sem.at[2])
    take_prec = pltpu.make_async_copy(prec_ref, prec_all.at[core], local_sem.at[3])
    take_innov = pltpu.make_async_copy(innov_ref, innov_all.at[core], local_sem.at[4])
    for copy in (take_lists, take_loc, take_pert, take_prec, take_innov):
        copy.start()

    barrier = pltpu.get_barrier_semaphore()
    for peer in z_peers:
        pl.semaphore_signal(barrier, inc=1, device_id=(s, peer), device_id_type=MESH)
    for peer in s_peers:
        pl.semaphore_signal(barrier, inc=1, device_id=(peer, m), device_id_type=MESH)
    pl.semaphore_wait(barrier, len(z_peers) + len(s_peers))

    def span(h):
        return pl.ds(h * part, part)

    def to_z(peer, h):
        return remote(
            pert_ref.at[:, span(h)], pert_all.at[core, m, :, span(h)],
            z_send.at[peer, h], z_recv.at[m, h], (s, peer),
        )

    def from_z(peer, h):
        return remote(
            pert_ref.at[:, span(h)], pert_all.at[core, peer, :, span(h)],
            z_send.at[m, h], z_recv.at[peer, h], (s, peer),
        )

    def across(owner, h, src):
        return remote(
            src, pert_all.at[core, owner, :, span(h)],
            core_send.at[owner, h], core_recv.at[owner, h], sibling,
        )

    def from_across(owner, h):
        there = pert_all.at[1 - core, owner, :, span(h)]
        return remote(there, there, core_send.at[owner, h], core_recv.at[owner, h], sibling)

    for h in range(PARTS):
        for peer in z_peers:
            to_z(peer, h).start()
    extra_out = [
        remote(prec_ref, prec_all.at[core], extra_send.at[0], extra_recv.at[0], sibling),
        remote(innov_ref, innov_all.at[core], extra_send.at[1], extra_recv.at[1], sibling),
    ]
    extra_in = [
        remote(prec_ref, prec_all.at[1 - core], extra_send.at[0], extra_recv.at[0], sibling),
        remote(innov_ref, innov_all.at[1 - core], extra_send.at[1], extra_recv.at[1], sibling),
    ]
    for copy in extra_out:
        copy.start()
    for h in range(PARTS):
        across(m, h, pert_ref.at[:, span(h)]).start()

    take_lists.wait()
    take_loc.wait()
    loc_f32[...] = loc_ref[...].astype(jnp.float32)
    for parity in range(CORES):
        def pick_rows(t, carry):
            for g in range(nm):
                row = send_ref[g, t * CORES + parity] + g * group_len
                rows_list[parity, pl.ds(t * nm + g, 1), :] = lists_ref[pl.ds(row, 1), :]
                rows_loc[parity, pl.ds(t * nm + g, 1), :] = loc_f32[pl.ds(row, 1), :]
            return carry

        lax.fori_loop(0, nc, pick_rows, 0, unroll=nc <= 4)
        spots = rows_list[parity]
        high = lax.shift_right_logical(spots, 7).astype(jnp.float32)
        low = jnp.bitwise_and(spots, LANES - 1).astype(jnp.float32)
        message[parity, :, 0:lobs] = high.astype(jnp.bfloat16)
        message[parity, :, lobs : 2 * lobs] = low.astype(jnp.bfloat16)
        message[parity, :, 2 * lobs : 3 * lobs] = rows_loc[parity].astype(jnp.bfloat16)
    pick_row = lax.broadcasted_iota(jnp.int32, (table.shape[1], LANES), 0)
    tile_of = jnp.zeros((table.shape[1], LANES), jnp.int32)
    group_of = jnp.zeros((table.shape[1], LANES), jnp.int32)
    for p in range(picks):
        q = m * picks + p
        slot = src_ref[q % 2, q // 2]
        tile_of = jnp.where(pick_row == p, slot % ns, tile_of)
        group_of = jnp.where(pick_row == p, slot // ns, group_of)
    for parity in range(CORES):
        message[parity, :, 3 * lobs : 3 * lobs + LANES] = (
            tile_of.astype(jnp.float32).astype(jnp.bfloat16)
        )
        message[parity, :, 3 * lobs + LANES :] = group_of.astype(jnp.float32).astype(jnp.bfloat16)

    def list_to(peer):
        return remote(
            message.at[peer % CORES], table.at[s], list_send.at[peer], list_recv.at[s], (peer, m)
        )

    def list_from(peer):
        return remote(
            message.at[core], table.at[peer], list_send.at[peer], list_recv.at[peer], (peer, m)
        )

    for peer in s_peers:
        list_to(peer).start()
    table[s] = message[core]
    gram[...] = jnp.zeros_like(gram)
    for peer in s_peers:
        list_from(peer).wait_recv()

    deep = nc * ROWS16
    per_tile = table.shape[1]
    tiles_col, rows_col = [], []
    for t in range(nc):
        cut = table[t * CORES + core, 0:ROWS16, 3 * lobs :].astype(jnp.float32)
        tiles_col.append(cut[:, 0:1])
        rows_col.append(cut[:, LANES : LANES + 1] + float(t * nm))
    tiles_col = jnp.concatenate(tiles_col, axis=0).astype(jnp.int32)
    rows_col = jnp.concatenate(rows_col, axis=0).astype(jnp.int32)
    at_row = lax.broadcasted_iota(jnp.int32, (deep, per_tile), 1) == rows_col

    def select(t):
        hot = jnp.where(jnp.logical_and(at_row, tiles_col == t), 1.0, 0.0).astype(jnp.bfloat16)
        return mm(hot, table[t, :, 0 : 3 * lobs])

    if ns <= 8:
        total = select(0)
        for t in range(1, ns):
            total += select(t)
        chosen[...] = total
    else:
        chosen[...] = jnp.zeros_like(chosen)

        def select_step(t, carry):
            chosen[...] += select(t)
            return carry

        lax.fori_loop(0, ns, select_step, 0)
    shift = (tiles_col - 1) * tile_his - chip * (CORES * tile_his)
    spots = chosen[:, 0:lobs] + shift.astype(jnp.float32)
    around = float(ns * tile_his)
    spots = jnp.where(spots < 0.0, spots + around, spots)
    chosen[:, 0:lobs] = jnp.where(spots >= around, spots - around, spots)

    for copy in (take_prec, take_innov):
        copy.wait()
    for copy in extra_in:
        copy.wait_recv()
    innov_f32[...] = innov_all[...].astype(jnp.float32)
    his = CORES * tile_his
    hi_iota = lax.broadcasted_iota(jnp.int32, (his, lobs), 0).astype(jnp.float32)
    lo_iota = lax.broadcasted_iota(jnp.int32, (LANES, lobs), 0).astype(jnp.float32)
    prec = jnp.concatenate([prec_all[i].astype(jnp.float32) for i in range(CORES)], axis=0)
    contract = (((1,), (1,)), ((), ()))

    def spread(t, carry):
        for p in range(picks):
            row = pl.ds(t * ROWS16 + p, 1)
            high, low = chosen[row, 0:lobs], chosen[row, lobs : 2 * lobs]
            taper = chosen[row, 2 * lobs : 3 * lobs]
            hi_hot = jnp.where(hi_iota == high, taper, 0.0).astype(jnp.bfloat16)
            lo_hot = jnp.where(lo_iota == low, 1.0, 0.0).astype(jnp.bfloat16)
            dense[t * picks + p] = prec * lax.dot_general(
                hi_hot, lo_hot, contract, preferred_element_type=jnp.float32
            )
        return carry

    lax.fori_loop(0, nc, spread, 0)

    per = CHUNK // LANES

    def take_chunk(tile, first):
        where = pl.ds(pl.multiple_of(first, CHUNK), CHUNK)
        wide = jnp.concatenate(
            [pert_all[tile, i, :, where].astype(jnp.float32) for i in range(nm)], axis=0
        )
        line = jnp.concatenate(
            [innov_f32[tile, pl.ds(first // LANES + j, 1), :] for j in range(per)], axis=1
        )
        line = jnp.where(lax.broadcasted_iota(jnp.int32, (ROWS16, CHUNK), 0) == 0, line, 0.0)
        return wide, jnp.concatenate([wide, line], axis=0).astype(jnp.bfloat16)

    def add_tile(t, tile, first, wide, cells):
        for p in range(picks):
            b = t * picks + p
            parts = []
            for j in range(per):
                at = pl.ds(tile * tile_his + first // LANES + j, 1)
                parts.append(wide[:, j * LANES : (j + 1) * LANES] * dense[b, at, :])
            high, low = split(jnp.concatenate(parts, axis=1))
            gram[b, :, : cells.shape[0]] += lax.dot_general(
                high, cells, contract, preferred_element_type=jnp.float32
            ) + lax.dot_general(low, cells, contract, preferred_element_type=jnp.float32)

    def add_part(tile, h):
        def chunk_step(c, carry):
            first = h * part + c * CHUNK
            wide, cells = take_chunk(tile, first)

            def pick_step(t, carry):
                add_tile(t, tile, first, wide, cells)
                return carry

            lax.fori_loop(0, nc, pick_step, 0, unroll=nc <= 4)
            return carry

        lax.fori_loop(0, part // CHUNK, chunk_step, 0)

    half = members // 2
    turn = half + 1
    low_cols = lax.broadcasted_iota(jnp.int32, (half, LANES), 1)

    def pack(t):
        for p in range(picks):
            b = t * picks + p
            under = jnp.where(low_cols >= half, gram[b, half:, :], 0.0)
            gram_out[t, p] = gram[b, :half, :] + pltpu.roll(under, turn, 1)

    def arrive(h):
        for peer in z_peers:
            from_z(peer, h).wait_recv()
            across(peer, h, pert_all.at[core, peer, :, span(h)]).start()

    def arrive_across(h):
        for i in range(nm):
            from_across(i, h).wait_recv()

    def gram_to(peer):
        return remote(
            gram_out.at[peer], gram_in.at[chip],
            gram_send.at[peer], gram_recv.at[chip], (peer * CORES + core, m),
        )

    def gram_from(peer):
        return remote(
            gram_out.at[peer], gram_in.at[peer],
            gram_send.at[peer], gram_recv.at[peer], (peer * CORES + core, m),
        )

    take_pert.wait()
    for h in range(PARTS):
        arrive(h)
        add_part(core, h)
        arrive_across(h)
        if h + 1 < PARTS or nc > 4 or part > CHUNK:
            add_part(1 - core, h)

    if nc <= 4 and part <= CHUNK:
        first = (PARTS - 1) * part
        wide, cells = take_chunk(1 - core, first)
        for t in chips[::-1] + [chip]:
            add_tile(t, 1 - core, first, wide, cells)
            pack(t)
            if t is not chip:
                gram_to(t).start()
    else:

        def pack_step(t, carry):
            pack(t)
            return carry

        lax.fori_loop(0, nc, pack_step, 0)
        for peer in reversed(chips):
            gram_to(peer).start()

    rows = lax.broadcasted_iota(jnp.int32, (members, LANES), 0)
    cols = lax.broadcasted_iota(jnp.int32, (members, LANES), 1)
    on_diag = rows == cols
    half3 = jnp.where(on_diag, 1.5, 0.0)

    for peer in chips:
        gram_from(peer).wait_recv()
    for p in range(picks):
        top = gram_out[chip, p]
        for peer in chips:
            top += gram_in[peer, p]
        under = pltpu.roll(top, LANES - turn, 1)
        filler = jnp.zeros((LANES - half, LANES), jnp.float32)
        flipped = jnp.concatenate([top, filler], axis=0).T[half : 2 * half]
        both = jnp.concatenate([top, jnp.where(low_cols < half, flipped, under)], axis=0)
        pulled[p] = jnp.sum(jnp.where(cols == members, both, 0.0), axis=1, keepdims=True)
        matrix = jnp.where(cols < members, both, 0.0) + jnp.where(on_diag, members - 1.0, 0.0)
        scale = jnp.sum(
            jnp.sum(jnp.where(on_diag, matrix, 0.0), axis=1, keepdims=True), axis=0, keepdims=True
        )
        scales[p] = jnp.broadcast_to(scale, (1, LANES))
        start = matrix / scale
        correction = half3 - 0.5 * start
        root[p] = halves(mm(left_side(start), right_side(correction)))
        inverse[p] = correction

    def newton(step, carry):
        corrections, pairs = [], []
        filler = jnp.zeros((LANES - members, 2 * LANES), jnp.bfloat16)
        for p in range(picks):
            r, z = left_side(root[p]), left_side(inverse[p])
            rhs = jnp.concatenate([r, filler, r, filler], axis=0)
            corrections.append(half3 - 0.5 * halves(mm(z, rhs)))
            pairs.append(jnp.concatenate([r, z], axis=0))
        for p in range(picks):
            both = halves(mm(pairs[p], right_side(corrections[p])))
            root[p] = both[:members]
            inverse[p] = both[members:]
        return carry

    lax.fori_loop(0, ITERS - 1, newton, 0)

    sums = [jnp.zeros((members, LANES), jnp.float32) for _ in range(slots)]
    base = (m * picks) // 2
    for p in range(picks):
        z = inverse[p]
        scale = scales[p]
        half_way = jnp.sum(z * pulled[p], axis=0, keepdims=True)
        mean_weight = jnp.sum(z * half_way, axis=1, keepdims=True) / scale[:, :1]
        trans = jnp.sqrt((members - 1.0) / scale) * z + mean_weight
        trans = trans.astype(jnp.bfloat16).astype(jnp.float32)
        q = m * picks + p
        o = q // 2
        frac = frac_ref[o]
        weight = jnp.where(q % 2 == 0, 1.0 - frac, frac)
        for j in range(max(0, p // 2), min(slots, p // 2 + 2)):
            sums[j] += jnp.where(o - base == j, weight, 0.0) * trans
    for j in range(slots):
        mixed[j] = sums[j].astype(jnp.bfloat16)

    def mix_to(peer):
        return remote(mixed, mixed_in.at[m], mix_send.at[peer], mix_recv.at[m], (s, peer))

    def mix_from(peer):
        return remote(mixed, mixed_in.at[peer], mix_send.at[peer], mix_recv.at[peer], (s, peer))

    for peer in z_peers:
        mix_to(peer).start()
    mixed_in[m] = mixed[...]
    for peer in chips:
        gram_to(peer).wait_send()
    for peer in s_peers:
        list_to(peer).wait_send()
    for copy in extra_out:
        copy.wait_send()
    for h in range(PARTS):
        for peer in z_peers:
            to_z(peer, h).wait_send()
            across(peer, h, pert_all.at[core, peer, :, span(h)]).wait_send()
        across(m, h, pert_ref.at[:, span(h)]).wait_send()
    for peer in z_peers:
        mix_from(peer).wait_recv()
    for o in range(oblocks):
        total = None
        for owner in range(nm):
            j = o - (owner * picks) // 2
            if 0 <= j and o <= (owner * picks + picks - 1) // 2:
                term = mixed_in[owner, j].astype(jnp.float32)
                total = term if total is None else total + term
        out_ref[o] = total.astype(jnp.bfloat16)
    for peer in z_peers:
        mix_to(peer).wait_send()


def mixed_weights(send, src, frac, lists, loc, pert, prec, innov):
    ns, nm = lax.axis_size("space"), lax.axis_size("member")
    shard, tile_obs = pert.shape
    members = shard * nm
    oblocks = src.shape[1]
    nc = ns // CORES
    picks = 2 * oblocks // nm
    assert picks * nm == 2 * oblocks and picks <= ROWS16
    slots = picks // 2 + picks % 2
    his = tile_obs // LANES
    lobs = lists.shape[1]
    vmem = pl.BlockSpec(memory_space=pltpu.VMEM)
    hbm = pl.BlockSpec(memory_space=pl.ANY)
    smem = pl.BlockSpec(memory_space=pltpu.SMEM)
    dma = pltpu.SemaphoreType.DMA
    bf16, f32 = jnp.bfloat16, jnp.float32
    blocks = lambda n, kind: pltpu.VMEM((n, members, LANES), kind)
    wide = 3 * lobs + 2 * LANES
    big = nc * nm * ns * wide * 2 > 4 * 2**20
    return pl.pallas_call(
        functools.partial(letkf_kernel, ns, nm, picks),
        in_specs=[smem, smem, smem, hbm, hbm, hbm, hbm, hbm],
        out_specs=vmem,
        out_shape=jax.ShapeDtypeStruct((oblocks, members, LANES), bf16),
        scratch_shapes=[
            pltpu.VMEM(lists.shape, lists.dtype),
            pltpu.VMEM(loc.shape, loc.dtype),
            pltpu.VMEM(loc.shape, f32),
            pltpu.VMEM((CORES, nm, shard, tile_obs), bf16),
            pltpu.VMEM((CORES, his, LANES), bf16),
            pltpu.VMEM((CORES, his, LANES), bf16),
            pltpu.VMEM((CORES, his, LANES), f32),
            pltpu.VMEM((CORES, nc * nm, lobs), lists.dtype),
            pltpu.VMEM((CORES, nc * nm, lobs), f32),
            pltpu.VMEM((CORES, nc * nm, wide), bf16),
            pltpu.VMEM((ns, nc * nm, wide), bf16),
            pltpu.VMEM((nc * ROWS16, 3 * lobs), f32),
            pltpu.VMEM((nc * picks, CORES * his, LANES), f32),
            blocks(nc * picks, f32),
            pltpu.VMEM((nc, picks, members // 2, LANES), f32),
            pltpu.VMEM((nc, picks, members // 2, LANES), f32),
            blocks(picks, f32),
            blocks(picks, f32),
            pltpu.VMEM((picks, members, 1), f32),
            pltpu.VMEM((picks, 1, LANES), f32),
            blocks(slots, bf16),
            pltpu.VMEM((nm, slots, members, LANES), bf16),
            dma((5,)), dma((nm, PARTS)), dma((nm, PARTS)), dma((nm, PARTS)), dma((nm, PARTS)),
            dma((2,)), dma((2,)), dma((ns,)), dma((ns,)), dma((nc,)), dma((nc,)),
            dma((nm,)), dma((nm,)),
        ],
        compiler_params=pltpu.CompilerParams(
            collective_id=0, has_side_effects=True,
            vmem_limit_bytes=56 * 2**20 if big else None,
        ),
        name="mixed_weights",
    )(send, src, frac, lists, loc, pert, prec, innov)


def apply_weights(ensemble, mixed):
    ens_mean = jnp.mean(ensemble, axis=0, dtype=jnp.float32)
    deviation = (ensemble.astype(jnp.float32) - ens_mean[None]).astype(jnp.bfloat16)
    product = jnp.einsum("jol,oji->iol", deviation, mixed, preferred_element_type=jnp.float32)
    return (ens_mean[None] + product).astype(jnp.bfloat16)


def shards(
    obs_pert,
    innovation,
    obs_prec,
    obs_lists,
    loc_weight,
    send_rows,
    ocean_src,
    ocean_frac,
    ocean_ens,
):
    mixed = mixed_weights(
        send_rows[0], ocean_src.T, ocean_frac, obs_lists, loc_weight, obs_pert,
        obs_prec.reshape(-1, LANES), innovation.reshape(-1, LANES),
    )
    mixed = mixed[:, :, : ocean_ens.shape[0]]
    return apply_weights(ocean_ens, mixed)


def solution(mesh):
    return jax.shard_map(
        shards,
        mesh=mesh,
        in_specs=(
            P("member", "space"),
            P("space"),
            P("space"),
            P("space", None),
            P("space", None),
            P("space", None, None),
            P("space", None),
            P("space"),
            P(None, "space", "member"),
        ),
        out_specs=P(None, "space", "member"),
        check_vma=False,
    )
```

```python
import functools

import jax
import jax.numpy as jnp
from jax import lax
from jax.experimental import pallas as pl
from jax.experimental.pallas import tpu as pltpu
from jax.sharding import PartitionSpec as P

ITERS = 12
LANES = 128
CHUNK = 1024
CORES = 2
ROWS16 = 16
PARTS = 2


def split(value):
    high = value.astype(jnp.bfloat16)
    low = (value - high.astype(jnp.float32)).astype(jnp.bfloat16)
    return high, low


def left_side(value):
    return jnp.concatenate(split(value), axis=1)


def right_side(value):
    pair = left_side(value)
    filler = jnp.zeros((LANES - pair.shape[0], pair.shape[1]), jnp.bfloat16)
    return jnp.concatenate([pair, filler, pair, filler], axis=0)


def halves(product):
    return product[:, :LANES] + product[:, LANES:]


def mm(lhs, rhs):
    return jnp.dot(lhs, rhs, preferred_element_type=jnp.float32)


def xor(value, flip, size):
    result, bit = 0, 1
    while bit < size:
        own = (value // bit) % 2
        result = result + (1 - own if flip & bit else own) * bit
        bit *= 2
    return result


MESH = pl.DeviceIdType.MESH


def remote(src, dst, send_sem, recv_sem, device):
    return pltpu.make_async_remote_copy(
        src_ref=src, dst_ref=dst, send_sem=send_sem, recv_sem=recv_sem,
        device_id=device, device_id_type=MESH,
    )


def letkf_kernel(
    ns, nm, picks,
    send_ref, src_ref, frac_ref, lists_hbm, loc_hbm, pert_ref, prec_ref, innov_ref, ens_hbm, out_ref,
    lists_ref, loc_ref, loc_f32, pert_all, prec_all, innov_all, innov_f32, rows_list, rows_loc,
    message, table, chosen, dense, gram, gram_out, gram_in, root, inverse, pulled, scales, mixed, mixed_in, ens, ens_mean,
    local_sem, z_send, z_recv, core_send, core_recv, extra_send, extra_recv,
    list_send, list_recv, gram_send, gram_recv, mix_send, mix_recv,
):
    s = lax.axis_index("space")
    m = lax.axis_index("member")
    nc = ns // CORES
    core, chip = s % CORES, s // CORES
    sibling = (s + 1 - 2 * core, m)
    members = pert_ref.shape[0] * nm
    tile_obs = pert_ref.shape[1]
    tile_his = tile_obs // LANES
    part = tile_obs // PARTS
    group_len = lists_ref.shape[0] // nm
    lobs = lists_ref.shape[1]
    oblocks = out_ref.shape[0]
    slots = mixed.shape[0]
    z_peers = [xor(m, k, nm) for k in range(1, nm)]
    chips = [xor(chip, k, nc) for k in range(1, nc)]
    s_peers = [lax.rem(s + k, ns) for k in range(1, ns)]

    take_lists = pltpu.make_async_copy(lists_hbm, lists_ref, local_sem.at[0])
    take_loc = pltpu.make_async_copy(loc_hbm, loc_ref, local_sem.at[1])
    take_pert = pltpu.make_async_copy(pert_ref, pert_all.at[core, m], local_sem.at[2])
    take_prec = pltpu.make_async_copy(prec_ref, prec_all.at[core], local_sem.at[3])
    take_innov = pltpu.make_async_copy(innov_ref, innov_all.at[core], local_sem.at[4])
    take_ens = pltpu.make_async_copy(ens_hbm, ens, local_sem.at[5])
    for copy in (take_lists, take_loc, take_pert, take_prec, take_innov, take_ens):
        copy.start()

    barrier = pltpu.get_barrier_semaphore()
    for peer in z_peers:
        pl.semaphore_signal(barrier, inc=1, device_id=(s, peer), device_id_type=MESH)
    for peer in s_peers:
        pl.semaphore_signal(barrier, inc=1, device_id=(peer, m), device_id_type=MESH)
    pl.semaphore_wait(barrier, len(z_peers) + len(s_peers))

    def span(h):
        return pl.ds(h * part, part)

    def to_z(peer, h):
        return remote(
            pert_ref.at[:, span(h)], pert_all.at[core, m, :, span(h)],
            z_send.at[peer, h], z_recv.at[m, h], (s, peer),
        )

    def from_z(peer, h):
        return remote(
            pert_ref.at[:, span(h)], pert_all.at[core, peer, :, span(h)],
            z_send.at[m, h], z_recv.at[peer, h], (s, peer),
        )

    def across(owner, h, src):
        return remote(
            src, pert_all.at[core, owner, :, span(h)],
            core_send.at[owner, h], core_recv.at[owner, h], sibling,
        )

    def from_across(owner, h):
        there = pert_all.at[1 - core, owner, :, span(h)]
        return remote(there, there, core_send.at[owner, h], core_recv.at[owner, h], sibling)

    for h in range(PARTS):
        for peer in z_peers:
            to_z(peer, h).start()
    extra_out = [
        remote(prec_ref, prec_all.at[core], extra_send.at[0], extra_recv.at[0], sibling),
        remote(innov_ref, innov_all.at[core], extra_send.at[1], extra_recv.at[1], sibling),
    ]
    extra_in = [
        remote(prec_ref, prec_all.at[1 - core], extra_send.at[0], extra_recv.at[0], sibling),
        remote(innov_ref, innov_all.at[1 - core], extra_send.at[1], extra_recv.at[1], sibling),
    ]
    for copy in extra_out:
        copy.start()
    for h in range(PARTS):
        across(m, h, pert_ref.at[:, span(h)]).start()

    take_lists.wait()
    take_loc.wait()
    loc_f32[...] = loc_ref[...].astype(jnp.float32)
    for parity in range(CORES):
        def pick_rows(t, carry):
            for g in range(nm):
                row = send_ref[g, t * CORES + parity] + g * group_len
                rows_list[parity, pl.ds(t * nm + g, 1), :] = lists_ref[pl.ds(row, 1), :]
                rows_loc[parity, pl.ds(t * nm + g, 1), :] = loc_f32[pl.ds(row, 1), :]
            return carry

        lax.fori_loop(0, nc, pick_rows, 0, unroll=nc <= 4)
        spots = rows_list[parity]
        high = lax.shift_right_logical(spots, 7).astype(jnp.float32)
        low = jnp.bitwise_and(spots, LANES - 1).astype(jnp.float32)
        message[parity, :, 0:lobs] = high.astype(jnp.bfloat16)
        message[parity, :, lobs : 2 * lobs] = low.astype(jnp.bfloat16)
        message[parity, :, 2 * lobs : 3 * lobs] = rows_loc[parity].astype(jnp.bfloat16)
    pick_row = lax.broadcasted_iota(jnp.int32, (table.shape[1], LANES), 0)
    tile_of = jnp.zeros((table.shape[1], LANES), jnp.int32)
    group_of = jnp.zeros((table.shape[1], LANES), jnp.int32)
    for p in range(picks):
        q = m * picks + p
        slot = src_ref[q % 2, q // 2]
        tile_of = jnp.where(pick_row == p, slot % ns, tile_of)
        group_of = jnp.where(pick_row == p, slot // ns, group_of)
    for parity in range(CORES):
        message[parity, :, 3 * lobs : 3 * lobs + LANES] = (
            tile_of.astype(jnp.float32).astype(jnp.bfloat16)
        )
        message[parity, :, 3 * lobs + LANES :] = group_of.astype(jnp.float32).astype(jnp.bfloat16)

    def list_to(peer):
        return remote(
            message.at[peer % CORES], table.at[s], list_send.at[peer], list_recv.at[s], (peer, m)
        )

    def list_from(peer):
        return remote(
            message.at[core], table.at[peer], list_send.at[peer], list_recv.at[peer], (peer, m)
        )

    for peer in s_peers:
        list_to(peer).start()
    table[s] = message[core]
    gram[...] = jnp.zeros_like(gram)
    for peer in s_peers:
        list_from(peer).wait_recv()

    deep = nc * ROWS16
    per_tile = table.shape[1]
    tiles_col, rows_col = [], []
    for t in range(nc):
        cut = table[t * CORES + core, 0:ROWS16, 3 * lobs :].astype(jnp.float32)
        tiles_col.append(cut[:, 0:1])
        rows_col.append(cut[:, LANES : LANES + 1] + float(t * nm))
    tiles_col = jnp.concatenate(tiles_col, axis=0).astype(jnp.int32)
    rows_col = jnp.concatenate(rows_col, axis=0).astype(jnp.int32)
    at_row = lax.broadcasted_iota(jnp.int32, (deep, per_tile), 1) == rows_col

    def select(t):
        hot = jnp.where(jnp.logical_and(at_row, tiles_col == t), 1.0, 0.0).astype(jnp.bfloat16)
        return mm(hot, table[t, :, 0 : 3 * lobs])

    if ns <= 8:
        total = select(0)
        for t in range(1, ns):
            total += select(t)
        chosen[...] = total
    else:
        chosen[...] = jnp.zeros_like(chosen)

        def select_step(t, carry):
            chosen[...] += select(t)
            return carry

        lax.fori_loop(0, ns, select_step, 0)
    shift = (tiles_col - 1) * tile_his - chip * (CORES * tile_his)
    spots = chosen[:, 0:lobs] + shift.astype(jnp.float32)
    around = float(ns * tile_his)
    spots = jnp.where(spots < 0.0, spots + around, spots)
    chosen[:, 0:lobs] = jnp.where(spots >= around, spots - around, spots)

    for copy in (take_prec, take_innov):
        copy.wait()
    for copy in extra_in:
        copy.wait_recv()
    innov_f32[...] = innov_all[...].astype(jnp.float32)
    his = CORES * tile_his
    hi_iota = lax.broadcasted_iota(jnp.int32, (his, lobs), 0).astype(jnp.float32)
    lo_iota = lax.broadcasted_iota(jnp.int32, (LANES, lobs), 0).astype(jnp.float32)
    prec = jnp.concatenate([prec_all[i].astype(jnp.float32) for i in range(CORES)], axis=0)
    contract = (((1,), (1,)), ((), ()))

    def spread(t, carry):
        for p in range(picks):
            row = pl.ds(t * ROWS16 + p, 1)
            high, low = chosen[row, 0:lobs], chosen[row, lobs : 2 * lobs]
            taper = chosen[row, 2 * lobs : 3 * lobs]
            hi_hot = jnp.where(hi_iota == high, taper, 0.0).astype(jnp.bfloat16)
            lo_hot = jnp.where(lo_iota == low, 1.0, 0.0).astype(jnp.bfloat16)
            dense[t * picks + p] = prec * lax.dot_general(
                hi_hot, lo_hot, contract, preferred_element_type=jnp.float32
            )
        return carry

    lax.fori_loop(0, nc, spread, 0)

    per = CHUNK // LANES

    def take_chunk(tile, first):
        where = pl.ds(pl.multiple_of(first, CHUNK), CHUNK)
        wide = jnp.concatenate(
            [pert_all[tile, i, :, where].astype(jnp.float32) for i in range(nm)], axis=0
        )
        line = jnp.concatenate(
            [innov_f32[tile, pl.ds(first // LANES + j, 1), :] for j in range(per)], axis=1
        )
        line = jnp.where(lax.broadcasted_iota(jnp.int32, (ROWS16, CHUNK), 0) == 0, line, 0.0)
        return wide, jnp.concatenate([wide, line], axis=0).astype(jnp.bfloat16)

    def add_tile(t, tile, first, wide, cells):
        for p in range(picks):
            b = t * picks + p
            parts = []
            for j in range(per):
                at = pl.ds(tile * tile_his + first // LANES + j, 1)
                parts.append(wide[:, j * LANES : (j + 1) * LANES] * dense[b, at, :])
            high, low = split(jnp.concatenate(parts, axis=1))
            gram[b, :, : cells.shape[0]] += lax.dot_general(
                high, cells, contract, preferred_element_type=jnp.float32
            ) + lax.dot_general(low, cells, contract, preferred_element_type=jnp.float32)

    def add_part(tile, h):
        def chunk_step(c, carry):
            first = h * part + c * CHUNK
            wide, cells = take_chunk(tile, first)

            def pick_step(t, carry):
                add_tile(t, tile, first, wide, cells)
                return carry

            lax.fori_loop(0, nc, pick_step, 0, unroll=nc <= 4)
            return carry

        lax.fori_loop(0, part // CHUNK, chunk_step, 0)

    half = members // 2
    turn = half + 1
    low_cols = lax.broadcasted_iota(jnp.int32, (half, LANES), 1)

    def pack(t):
        for p in range(picks):
            b = t * picks + p
            under = jnp.where(low_cols >= half, gram[b, half:, :], 0.0)
            gram_out[t, p] = gram[b, :half, :] + pltpu.roll(under, turn, 1)

    def arrive(h):
        for peer in z_peers:
            from_z(peer, h).wait_recv()
            across(peer, h, pert_all.at[core, peer, :, span(h)]).start()

    def arrive_across(h):
        for i in range(nm):
            from_across(i, h).wait_recv()

    def gram_to(peer):
        return remote(
            gram_out.at[peer], gram_in.at[chip],
            gram_send.at[peer], gram_recv.at[chip], (peer * CORES + core, m),
        )

    def gram_from(peer):
        return remote(
            gram_out.at[peer], gram_in.at[peer],
            gram_send.at[peer], gram_recv.at[peer], (peer * CORES + core, m),
        )

    take_ens.wait()

    def center(o, carry):
        wide = ens[o].astype(jnp.float32)
        mean = jnp.sum(wide, axis=0, keepdims=True) * (1.0 / members)
        ens_mean[o] = mean
        ens[o] = (wide - mean).astype(jnp.bfloat16)
        return carry

    lax.fori_loop(0, oblocks, center, 0)
    take_pert.wait()
    for h in range(PARTS):
        arrive(h)
        add_part(core, h)
        arrive_across(h)
        if h + 1 < PARTS or nc > 4 or part > CHUNK:
            add_part(1 - core, h)

    if nc <= 4 and part <= CHUNK:
        first = (PARTS - 1) * part
        wide, cells = take_chunk(1 - core, first)
        for t in chips[::-1] + [chip]:
            add_tile(t, 1 - core, first, wide, cells)
            pack(t)
            if t is not chip:
                gram_to(t).start()
    else:

        def pack_step(t, carry):
            pack(t)
            return carry

        lax.fori_loop(0, nc, pack_step, 0)
        for peer in reversed(chips):
            gram_to(peer).start()

    rows = lax.broadcasted_iota(jnp.int32, (members, LANES), 0)
    cols = lax.broadcasted_iota(jnp.int32, (members, LANES), 1)
    on_diag = rows == cols
    half3 = jnp.where(on_diag, 1.5, 0.0)

    for peer in chips:
        gram_from(peer).wait_recv()
    for p in range(picks):
        top = gram_out[chip, p]
        for peer in chips:
            top += gram_in[peer, p]
        under = pltpu.roll(top, LANES - turn, 1)
        filler = jnp.zeros((LANES - half, LANES), jnp.float32)
        flipped = jnp.concatenate([top, filler], axis=0).T[half : 2 * half]
        both = jnp.concatenate([top, jnp.where(low_cols < half, flipped, under)], axis=0)
        pulled[p] = jnp.sum(jnp.where(cols == members, both, 0.0), axis=1, keepdims=True)
        matrix = jnp.where(cols < members, both, 0.0) + jnp.where(on_diag, members - 1.0, 0.0)
        scale = jnp.sum(
            jnp.sum(jnp.where(on_diag, matrix, 0.0), axis=1, keepdims=True), axis=0, keepdims=True
        )
        scales[p] = jnp.broadcast_to(scale, (1, LANES))
        start = matrix / scale
        correction = half3 - 0.5 * start
        root[p] = halves(mm(left_side(start), right_side(correction)))
        inverse[p] = correction

    def newton(step, carry):
        corrections, pairs = [], []
        filler = jnp.zeros((LANES - members, 2 * LANES), jnp.bfloat16)
        for p in range(picks):
            r, z = left_side(root[p]), left_side(inverse[p])
            rhs = jnp.concatenate([r, filler, r, filler], axis=0)
            corrections.append(half3 - 0.5 * halves(mm(z, rhs)))
            pairs.append(jnp.concatenate([r, z], axis=0))
        for p in range(picks):
            both = halves(mm(pairs[p], right_side(corrections[p])))
            root[p] = both[:members]
            inverse[p] = both[members:]
        return carry

    lax.fori_loop(0, ITERS - 1, newton, 0)

    sums = [jnp.zeros((members, LANES), jnp.float32) for _ in range(slots)]
    base = (m * picks) // 2
    for p in range(picks):
        z = inverse[p]
        scale = scales[p]
        line = jnp.sum(jnp.where(on_diag, pulled[p], 0.0), axis=0, keepdims=True)
        half_way = jnp.sum(z * line, axis=1, keepdims=True)
        mean_weight = jnp.sum(z * half_way, axis=0, keepdims=True) / scale
        trans = jnp.sqrt((members - 1.0) / scale) * z + mean_weight
        trans = trans.astype(jnp.bfloat16).astype(jnp.float32)
        q = m * picks + p
        o = q // 2
        frac = frac_ref[o]
        weight = jnp.where(q % 2 == 0, 1.0 - frac, frac)
        for j in range(max(0, p // 2), min(slots, p // 2 + 2)):
            sums[j] += jnp.where(o - base == j, weight, 0.0) * trans
    for j in range(slots):
        mixed[j] = sums[j].astype(jnp.bfloat16)

    def mix_to(peer):
        return remote(mixed, mixed_in.at[m], mix_send.at[peer], mix_recv.at[m], (s, peer))

    def mix_from(peer):
        return remote(mixed, mixed_in.at[peer], mix_send.at[peer], mix_recv.at[peer], (s, peer))

    for peer in z_peers:
        mix_to(peer).start()
    mixed_in[m] = mixed[...]
    for peer in chips:
        gram_to(peer).wait_send()
    for peer in s_peers:
        list_to(peer).wait_send()
    for copy in extra_out:
        copy.wait_send()
    for h in range(PARTS):
        for peer in z_peers:
            to_z(peer, h).wait_send()
            across(peer, h, pert_all.at[core, peer, :, span(h)]).wait_send()
        across(m, h, pert_ref.at[:, span(h)]).wait_send()
    for peer in z_peers:
        mix_from(peer).wait_recv()
    def finish(o, owner, j):
        total = mixed_in[owner, j].astype(jnp.float32)
        if picks % 2 and j == slots - 1 and owner % 2 == 0:
            total += mixed_in[owner + 1, 0].astype(jnp.float32)
        weights = total.astype(jnp.bfloat16)[:, :members]
        out_ref[o] = (ens_mean[o] + mm(weights, ens[o])).astype(jnp.bfloat16)

    if oblocks <= 8:
        for o in range(oblocks):
            owner = (2 * o) // picks
            finish(o, owner, o - (owner * picks) // 2)
    else:

        def finish_step(owner, carry):
            for j in range(slots):
                finish(owner * slots + j, owner, j)
            return carry

        lax.fori_loop(0, nm, finish_step, 0)
    for peer in z_peers:
        mix_to(peer).wait_send()


def analysis(send, src, frac, lists, loc, pert, prec, innov, ens):
    ns, nm = lax.axis_size("space"), lax.axis_size("member")
    shard, tile_obs = pert.shape
    members = shard * nm
    oblocks = src.shape[1]
    nc = ns // CORES
    picks = 2 * oblocks // nm
    assert picks * nm == 2 * oblocks and picks <= ROWS16
    assert picks % 2 == 0 or oblocks <= 8
    slots = picks // 2 + picks % 2
    his = tile_obs // LANES
    lobs = lists.shape[1]
    vmem = pl.BlockSpec(memory_space=pltpu.VMEM)
    hbm = pl.BlockSpec(memory_space=pl.ANY)
    smem = pl.BlockSpec(memory_space=pltpu.SMEM)
    dma = pltpu.SemaphoreType.DMA
    bf16, f32 = jnp.bfloat16, jnp.float32
    blocks = lambda n, kind: pltpu.VMEM((n, members, LANES), kind)
    wide = 3 * lobs + 2 * LANES
    big = nc * nm * ns * wide * 2 > 4 * 2**20
    return pl.pallas_call(
        functools.partial(letkf_kernel, ns, nm, picks),
        in_specs=[smem, smem, smem, hbm, hbm, hbm, hbm, hbm, hbm],
        out_specs=vmem,
        out_shape=pltpu.VMEM(ens.shape, bf16),
        scratch_shapes=[
            pltpu.VMEM(lists.shape, lists.dtype),
            pltpu.VMEM(loc.shape, loc.dtype),
            pltpu.VMEM(loc.shape, f32),
            pltpu.VMEM((CORES, nm, shard, tile_obs), bf16),
            pltpu.VMEM((CORES, his, LANES), bf16),
            pltpu.VMEM((CORES, his, LANES), bf16),
            pltpu.VMEM((CORES, his, LANES), f32),
            pltpu.VMEM((CORES, nc * nm, lobs), lists.dtype),
            pltpu.VMEM((CORES, nc * nm, lobs), f32),
            pltpu.VMEM((CORES, nc * nm, wide), bf16),
            pltpu.VMEM((ns, nc * nm, wide), bf16),
            pltpu.VMEM((nc * ROWS16, 3 * lobs), f32),
            pltpu.VMEM((nc * picks, CORES * his, LANES), f32),
            blocks(nc * picks, f32),
            pltpu.VMEM((nc, picks, members // 2, LANES), f32),
            pltpu.VMEM((nc, picks, members // 2, LANES), f32),
            blocks(picks, f32),
            blocks(picks, f32),
            pltpu.VMEM((picks, members, 1), f32),
            pltpu.VMEM((picks, 1, LANES), f32),
            blocks(slots, bf16),
            pltpu.VMEM((nm, slots, members, LANES), bf16),
            pltpu.VMEM(ens.shape, bf16),
            pltpu.VMEM((oblocks, 1, ens.shape[2]), f32),
            dma((6,)), dma((nm, PARTS)), dma((nm, PARTS)), dma((nm, PARTS)), dma((nm, PARTS)),
            dma((2,)), dma((2,)), dma((ns,)), dma((ns,)), dma((nc,)), dma((nc,)),
            dma((nm,)), dma((nm,)),
        ],
        compiler_params=pltpu.CompilerParams(
            collective_id=0, has_side_effects=True,
            vmem_limit_bytes=56 * 2**20 if big else None,
        ),
        name="analysis",
    )(send, src, frac, lists, loc, pert, prec, innov, ens)


def shards(
    obs_pert,
    innovation,
    obs_prec,
    obs_lists,
    loc_weight,
    send_rows,
    ocean_src,
    ocean_frac,
    ocean_ens,
):
    result = analysis(
        send_rows[0], ocean_src.T, ocean_frac, obs_lists, loc_weight, obs_pert,
        obs_prec.reshape(-1, LANES), innovation.reshape(-1, LANES),
        ocean_ens.transpose(1, 0, 2),
    )
    return result.transpose(1, 0, 2)


def solution(mesh):
    return jax.shard_map(
        shards,
        mesh=mesh,
        in_specs=(
            P("member", "space"),
            P("space"),
            P("space"),
            P("space", None),
            P("space", None),
            P("space", None, None),
            P("space", None),
            P("space"),
            P(None, "space", "member"),
        ),
        out_specs=P(None, "space", "member"),
        check_vma=False,
    )
```

```python
import functools

import jax
import jax.numpy as jnp
from jax import lax
from jax.experimental import pallas as pl
from jax.experimental.pallas import tpu as pltpu
from jax.sharding import PartitionSpec as P

ITERS = 12
LANES = 128
CHUNK = 1024
CORES = 2
ROWS16 = 16
PARTS = 2


def split(value):
    high = value.astype(jnp.bfloat16)
    low = (value - high.astype(jnp.float32)).astype(jnp.bfloat16)
    return high, low


def left_side(value):
    return jnp.concatenate(split(value), axis=1)


def right_side(value):
    pair = left_side(value)
    filler = jnp.zeros((LANES - pair.shape[0], pair.shape[1]), jnp.bfloat16)
    return jnp.concatenate([pair, filler, pair, filler], axis=0)


def halves(product):
    return product[:, :LANES] + product[:, LANES:]


def mm(lhs, rhs):
    return jnp.dot(lhs, rhs, preferred_element_type=jnp.float32)


def xor(value, flip, size):
    result, bit = 0, 1
    while bit < size:
        own = (value // bit) % 2
        result = result + (1 - own if flip & bit else own) * bit
        bit *= 2
    return result


MESH = pl.DeviceIdType.MESH


def remote(src, dst, send_sem, recv_sem, device):
    return pltpu.make_async_remote_copy(
        src_ref=src, dst_ref=dst, send_sem=send_sem, recv_sem=recv_sem,
        device_id=device, device_id_type=MESH,
    )


def letkf_kernel(
    ns, nm, picks,
    send_ref, src_ref, frac_ref, lists_hbm, loc_hbm, pert_ref, prec_ref, innov_ref, ens_hbm, out_ref,
    lists_ref, loc_ref, loc_f32, pert_all, prec_all, innov_all, innov_f32, rows_list, rows_loc,
    message, table, chosen, dense, gram, gram_out, gram_in, root, inverse, pulled, scales, mixed, mixed_in, ens, ens_mean,
    local_sem, z_send, z_recv, core_send, core_recv, extra_send, extra_recv,
    list_send, list_recv, gram_send, gram_recv, mix_send, mix_recv,
):
    s = lax.axis_index("space")
    m = lax.axis_index("member")
    nc = ns // CORES
    core, chip = s % CORES, s // CORES
    sibling = (s + 1 - 2 * core, m)
    members = pert_ref.shape[0] * nm
    tile_obs = pert_ref.shape[1]
    tile_his = tile_obs // LANES
    part = tile_obs // PARTS
    group_len = lists_ref.shape[0] // nm
    lobs = lists_ref.shape[1]
    oblocks = out_ref.shape[0]
    slots = mixed.shape[0] // (members // 2)
    z_peers = [xor(m, k, nm) for k in range(1, nm)]
    chips = [xor(chip, k, nc) for k in range(1, nc)]
    s_peers = [lax.rem(s + k, ns) for k in range(1, ns)]

    take_lists = pltpu.make_async_copy(lists_hbm, lists_ref, local_sem.at[0])
    take_loc = pltpu.make_async_copy(loc_hbm, loc_ref, local_sem.at[1])
    take_pert = pltpu.make_async_copy(pert_ref, pert_all.at[core, m], local_sem.at[2])
    take_prec = pltpu.make_async_copy(prec_ref, prec_all.at[core], local_sem.at[3])
    take_innov = pltpu.make_async_copy(innov_ref, innov_all.at[core], local_sem.at[4])
    take_ens = pltpu.make_async_copy(ens_hbm, ens, local_sem.at[5])
    for copy in (take_lists, take_loc, take_pert, take_prec, take_innov, take_ens):
        copy.start()

    barrier = pltpu.get_barrier_semaphore()
    for peer in z_peers:
        pl.semaphore_signal(barrier, inc=1, device_id=(s, peer), device_id_type=MESH)
    for peer in s_peers:
        pl.semaphore_signal(barrier, inc=1, device_id=(peer, m), device_id_type=MESH)
    pl.semaphore_wait(barrier, len(z_peers) + len(s_peers))

    def span(h):
        return pl.ds(h * part, part)

    def to_z(peer, h):
        return remote(
            pert_ref.at[:, span(h)], pert_all.at[core, m, :, span(h)],
            z_send.at[peer, h], z_recv.at[m, h], (s, peer),
        )

    def from_z(peer, h):
        return remote(
            pert_ref.at[:, span(h)], pert_all.at[core, peer, :, span(h)],
            z_send.at[m, h], z_recv.at[peer, h], (s, peer),
        )

    def across(owner, h, src):
        return remote(
            src, pert_all.at[core, owner, :, span(h)],
            core_send.at[owner, h], core_recv.at[owner, h], sibling,
        )

    def from_across(owner, h):
        there = pert_all.at[1 - core, owner, :, span(h)]
        return remote(there, there, core_send.at[owner, h], core_recv.at[owner, h], sibling)

    for h in range(PARTS):
        for peer in z_peers:
            to_z(peer, h).start()
    extra_out = [
        remote(prec_ref, prec_all.at[core], extra_send.at[0], extra_recv.at[0], sibling),
        remote(innov_ref, innov_all.at[core], extra_send.at[1], extra_recv.at[1], sibling),
    ]
    extra_in = [
        remote(prec_ref, prec_all.at[1 - core], extra_send.at[0], extra_recv.at[0], sibling),
        remote(innov_ref, innov_all.at[1 - core], extra_send.at[1], extra_recv.at[1], sibling),
    ]
    for copy in extra_out:
        copy.start()
    for h in range(PARTS):
        across(m, h, pert_ref.at[:, span(h)]).start()

    take_lists.wait()
    take_loc.wait()
    loc_f32[...] = loc_ref[...].astype(jnp.float32)
    for parity in range(CORES):
        def pick_rows(t, carry):
            for g in range(nm):
                row = send_ref[g, t * CORES + parity] + g * group_len
                rows_list[parity, pl.ds(t * nm + g, 1), :] = lists_ref[pl.ds(row, 1), :]
                rows_loc[parity, pl.ds(t * nm + g, 1), :] = loc_f32[pl.ds(row, 1), :]
            return carry

        lax.fori_loop(0, nc, pick_rows, 0, unroll=nc <= 4)
        spots = rows_list[parity]
        high = lax.shift_right_logical(spots, 7).astype(jnp.float32)
        low = jnp.bitwise_and(spots, LANES - 1).astype(jnp.float32)
        message[parity, :, 0:lobs] = high.astype(jnp.bfloat16)
        message[parity, :, lobs : 2 * lobs] = low.astype(jnp.bfloat16)
        message[parity, :, 2 * lobs : 3 * lobs] = rows_loc[parity].astype(jnp.bfloat16)
    pick_row = lax.broadcasted_iota(jnp.int32, (table.shape[1], LANES), 0)
    tile_of = jnp.zeros((table.shape[1], LANES), jnp.int32)
    group_of = jnp.zeros((table.shape[1], LANES), jnp.int32)
    for p in range(picks):
        q = m * picks + p
        slot = src_ref[q % 2, q // 2]
        tile_of = jnp.where(pick_row == p, slot % ns, tile_of)
        group_of = jnp.where(pick_row == p, slot // ns, group_of)
    for parity in range(CORES):
        message[parity, :, 3 * lobs : 3 * lobs + LANES] = (
            tile_of.astype(jnp.float32).astype(jnp.bfloat16)
        )
        message[parity, :, 3 * lobs + LANES :] = group_of.astype(jnp.float32).astype(jnp.bfloat16)

    def list_to(peer):
        return remote(
            message.at[peer % CORES], table.at[s], list_send.at[peer], list_recv.at[s], (peer, m)
        )

    def list_from(peer):
        return remote(
            message.at[core], table.at[peer], list_send.at[peer], list_recv.at[peer], (peer, m)
        )

    for peer in s_peers:
        list_to(peer).start()
    table[s] = message[core]
    gram[...] = jnp.zeros_like(gram)
    for peer in s_peers:
        list_from(peer).wait_recv()

    deep = nc * ROWS16
    per_tile = table.shape[1]
    tiles_col, rows_col = [], []
    for t in range(nc):
        cut = table[t * CORES + core, 0:ROWS16, 3 * lobs :].astype(jnp.float32)
        tiles_col.append(cut[:, 0:1])
        rows_col.append(cut[:, LANES : LANES + 1] + float(t * nm))
    tiles_col = jnp.concatenate(tiles_col, axis=0).astype(jnp.int32)
    rows_col = jnp.concatenate(rows_col, axis=0).astype(jnp.int32)
    at_row = lax.broadcasted_iota(jnp.int32, (deep, per_tile), 1) == rows_col

    def select(t):
        hot = jnp.where(jnp.logical_and(at_row, tiles_col == t), 1.0, 0.0).astype(jnp.bfloat16)
        return mm(hot, table[t, :, 0 : 3 * lobs])

    if ns <= 8:
        total = select(0)
        for t in range(1, ns):
            total += select(t)
        chosen[...] = total
    else:
        chosen[...] = jnp.zeros_like(chosen)

        def select_step(t, carry):
            chosen[...] += select(t)
            return carry

        lax.fori_loop(0, ns, select_step, 0)
    shift = (tiles_col - 1) * tile_his - chip * (CORES * tile_his)
    spots = chosen[:, 0:lobs] + shift.astype(jnp.float32)
    around = float(ns * tile_his)
    spots = jnp.where(spots < 0.0, spots + around, spots)
    chosen[:, 0:lobs] = jnp.where(spots >= around, spots - around, spots)

    for copy in (take_prec, take_innov):
        copy.wait()
    for copy in extra_in:
        copy.wait_recv()
    innov_f32[...] = innov_all[...].astype(jnp.float32)
    his = CORES * tile_his
    hi_iota = lax.broadcasted_iota(jnp.int32, (his, lobs), 0).astype(jnp.float32)
    lo_iota = lax.broadcasted_iota(jnp.int32, (LANES, lobs), 0).astype(jnp.float32)
    prec = jnp.concatenate([prec_all[i].astype(jnp.float32) for i in range(CORES)], axis=0)
    contract = (((1,), (1,)), ((), ()))

    def spread(t, carry):
        for p in range(picks):
            row = pl.ds(t * ROWS16 + p, 1)
            high, low = chosen[row, 0:lobs], chosen[row, lobs : 2 * lobs]
            taper = chosen[row, 2 * lobs : 3 * lobs]
            hi_hot = jnp.where(hi_iota == high, taper, 0.0).astype(jnp.bfloat16)
            lo_hot = jnp.where(lo_iota == low, 1.0, 0.0).astype(jnp.bfloat16)
            dense[t * picks + p] = prec * lax.dot_general(
                hi_hot, lo_hot, contract, preferred_element_type=jnp.float32
            )
        return carry

    lax.fori_loop(0, nc, spread, 0)

    per = CHUNK // LANES

    def take_chunk(tile, first):
        where = pl.ds(pl.multiple_of(first, CHUNK), CHUNK)
        wide = jnp.concatenate(
            [pert_all[tile, i, :, where].astype(jnp.float32) for i in range(nm)], axis=0
        )
        line = jnp.concatenate(
            [innov_f32[tile, pl.ds(first // LANES + j, 1), :] for j in range(per)], axis=1
        )
        line = jnp.where(lax.broadcasted_iota(jnp.int32, (ROWS16, CHUNK), 0) == 0, line, 0.0)
        return wide, jnp.concatenate([wide, line], axis=0).astype(jnp.bfloat16)

    def add_tile(t, tile, first, wide, cells):
        for p in range(picks):
            b = t * picks + p
            parts = []
            for j in range(per):
                at = pl.ds(tile * tile_his + first // LANES + j, 1)
                parts.append(wide[:, j * LANES : (j + 1) * LANES] * dense[b, at, :])
            high, low = split(jnp.concatenate(parts, axis=1))
            gram[b, :, : cells.shape[0]] += lax.dot_general(
                high, cells, contract, preferred_element_type=jnp.float32
            ) + lax.dot_general(low, cells, contract, preferred_element_type=jnp.float32)

    def add_part(tile, h):
        def chunk_step(c, carry):
            first = h * part + c * CHUNK
            wide, cells = take_chunk(tile, first)

            def pick_step(t, carry):
                add_tile(t, tile, first, wide, cells)
                return carry

            lax.fori_loop(0, nc, pick_step, 0, unroll=nc <= 4)
            return carry

        lax.fori_loop(0, part // CHUNK, chunk_step, 0)

    half = members // 2
    turn = half + 1
    low_cols = lax.broadcasted_iota(jnp.int32, (half, LANES), 1)

    def pack(t):
        for p in range(picks):
            b = t * picks + p
            under = jnp.where(low_cols >= half, gram[b, half:, :], 0.0)
            gram_out[t, p] = gram[b, :half, :] + pltpu.roll(under, turn, 1)

    def arrive(h):
        for peer in z_peers:
            from_z(peer, h).wait_recv()
            across(peer, h, pert_all.at[core, peer, :, span(h)]).start()

    def arrive_across(h):
        for i in range(nm):
            from_across(i, h).wait_recv()

    def gram_to(peer):
        return remote(
            gram_out.at[peer], gram_in.at[chip],
            gram_send.at[peer], gram_recv.at[chip], (peer * CORES + core, m),
        )

    def gram_from(peer):
        return remote(
            gram_out.at[peer], gram_in.at[peer],
            gram_send.at[peer], gram_recv.at[peer], (peer * CORES + core, m),
        )

    take_ens.wait()

    def center(o, carry):
        wide = ens[o].astype(jnp.float32)
        mean = jnp.sum(wide, axis=0, keepdims=True) * (1.0 / members)
        ens_mean[o] = mean
        ens[o] = (wide - mean).astype(jnp.bfloat16)
        return carry

    lax.fori_loop(0, oblocks, center, 0)
    take_pert.wait()
    for h in range(PARTS):
        arrive(h)
        add_part(core, h)
        arrive_across(h)
        if h + 1 < PARTS or nc > 4 or part > CHUNK:
            add_part(1 - core, h)

    if nc <= 4 and part <= CHUNK:
        first = (PARTS - 1) * part
        wide, cells = take_chunk(1 - core, first)
        for t in chips[::-1] + [chip]:
            add_tile(t, 1 - core, first, wide, cells)
            pack(t)
            if t is not chip:
                gram_to(t).start()
    else:

        def pack_step(t, carry):
            pack(t)
            return carry

        lax.fori_loop(0, nc, pack_step, 0)
        for peer in reversed(chips):
            gram_to(peer).start()

    rows = lax.broadcasted_iota(jnp.int32, (members, LANES), 0)
    cols = lax.broadcasted_iota(jnp.int32, (members, LANES), 1)
    on_diag = rows == cols
    half3 = jnp.where(on_diag, 1.5, 0.0)

    for peer in chips:
        gram_from(peer).wait_recv()
    filler = jnp.zeros((LANES - half, LANES), jnp.float32)
    for p in range(picks):
        top = gram_out[chip, p]
        for peer in chips:
            top += gram_in[peer, p]
        under = pltpu.roll(top, LANES - turn, 1)
        flipped = jnp.concatenate([top, filler], axis=0).T[half : 2 * half]
        both = jnp.concatenate([top, jnp.where(low_cols < half, flipped, under)], axis=0)
        pulled[p] = jnp.sum(jnp.where(cols == members, both, 0.0), axis=1, keepdims=True)
        matrix = jnp.where(cols < members, both, 0.0) + jnp.where(on_diag, members - 1.0, 0.0)
        scale = jnp.sum(
            jnp.sum(jnp.where(on_diag, matrix, 0.0), axis=1, keepdims=True), axis=0, keepdims=True
        )
        scales[p] = jnp.broadcast_to(scale, (1, LANES))
        start = matrix / scale
        correction = half3 - 0.5 * start
        root[p] = halves(mm(left_side(start), right_side(correction)))
        inverse[p] = correction

    def newton(step, carry):
        corrections, pairs = [], []
        space = jnp.zeros((LANES - members, 2 * LANES), jnp.bfloat16)
        for p in range(picks):
            r, z = left_side(root[p]), left_side(inverse[p])
            rhs = jnp.concatenate([r, space, r, space], axis=0)
            corrections.append(half3 - 0.5 * halves(mm(z, rhs)))
            pairs.append(jnp.concatenate([r, z], axis=0))
        for p in range(picks):
            both = halves(mm(pairs[p], right_side(corrections[p])))
            root[p] = both[:members]
            inverse[p] = both[members:]
        return carry

    lax.fori_loop(0, ITERS - 1, newton, 0)

    sums = [jnp.zeros((members, LANES), jnp.float32) for _ in range(slots)]
    means = [jnp.zeros((members, 1), jnp.float32) for _ in range(slots)]
    base = (m * picks) // 2
    for p in range(picks):
        z = inverse[p]
        scale = scales[p]
        half_way = jnp.sum(z * pulled[p], axis=0, keepdims=True)
        mean_weight = jnp.sum(z * half_way, axis=1, keepdims=True) / scale[:, :1]
        trans = jnp.sqrt((members - 1.0) / scale) * z
        q = m * picks + p
        o = q // 2
        frac = frac_ref[o]
        weight = jnp.where(q % 2 == 0, 1.0 - frac, frac)
        for j in range(max(0, p // 2), min(slots, p // 2 + 2)):
            share = jnp.where(o - base == j, weight, 0.0)
            sums[j] += share * trans
            means[j] += share * mean_weight
    for j in range(slots):
        under = jnp.where(low_cols < half, 0.0, jnp.where(low_cols < members, sums[j][half:], 0.0))
        packed = sums[j][:half] + pltpu.roll(under, half, 1)
        high = means[j].astype(jnp.bfloat16).astype(jnp.float32)
        tails = (high, means[j] - high)
        for k in range(4):
            tail = tails[k // 2][(k % 2) * half : (k % 2 + 1) * half]
            packed = jnp.where(low_cols == members + half + k, tail, packed)
        mixed[j * half : (j + 1) * half, :] = packed.astype(jnp.bfloat16)

    def mix_to(peer):
        return remote(mixed, mixed_in.at[m], mix_send.at[peer], mix_recv.at[m], (s, peer))

    def mix_from(peer):
        return remote(mixed, mixed_in.at[peer], mix_send.at[peer], mix_recv.at[peer], (s, peer))

    for peer in z_peers:
        mix_to(peer).start()
    mixed_in[m] = mixed[...]
    for peer in chips:
        gram_to(peer).wait_send()
    for peer in s_peers:
        list_to(peer).wait_send()
    for copy in extra_out:
        copy.wait_send()
    for h in range(PARTS):
        for peer in z_peers:
            to_z(peer, h).wait_send()
            across(peer, h, pert_all.at[core, peer, :, span(h)]).wait_send()
        across(m, h, pert_ref.at[:, span(h)]).wait_send()
    for peer in z_peers:
        mix_from(peer).wait_recv()
    def finish(o, owner, j):
        total = mixed_in[owner, j * half : (j + 1) * half].astype(jnp.float32)
        if picks % 2 and j == slots - 1 and owner % 2 == 0:
            total += mixed_in[owner + 1, 0:half].astype(jnp.float32)
        flipped = jnp.concatenate([total, filler], axis=0).T[half : 2 * half]
        under = jnp.where(low_cols < half, flipped, pltpu.roll(total, LANES - half, 1))
        first = members + half
        tail = total[:, first : first + 2] + total[:, first + 2 : first + 4]
        tail = jnp.concatenate([tail[:, 0:1], tail[:, 1:2]], axis=0)
        line = jnp.sum(jnp.where(on_diag, tail, 0.0), axis=0, keepdims=True)
        weights = jnp.concatenate([total, under], axis=0) + line
        weights = weights.astype(jnp.bfloat16)[:, :members]
        out_ref[o] = (ens_mean[o] + mm(weights, ens[o])).astype(jnp.bfloat16)

    if oblocks <= 8:
        for o in range(oblocks):
            owner = (2 * o) // picks
            finish(o, owner, o - (owner * picks) // 2)
    else:

        def finish_step(owner, carry):
            for j in range(slots):
                finish(owner * slots + j, owner, j)
            return carry

        lax.fori_loop(0, nm, finish_step, 0)
    for peer in z_peers:
        mix_to(peer).wait_send()


def analysis(send, src, frac, lists, loc, pert, prec, innov, ens):
    ns, nm = lax.axis_size("space"), lax.axis_size("member")
    shard, tile_obs = pert.shape
    members = shard * nm
    oblocks = src.shape[1]
    nc = ns // CORES
    picks = 2 * oblocks // nm
    assert picks * nm == 2 * oblocks and picks <= ROWS16
    assert picks % 2 == 0 or oblocks <= 8
    slots = picks // 2 + picks % 2
    his = tile_obs // LANES
    lobs = lists.shape[1]
    vmem = pl.BlockSpec(memory_space=pltpu.VMEM)
    hbm = pl.BlockSpec(memory_space=pl.ANY)
    smem = pl.BlockSpec(memory_space=pltpu.SMEM)
    dma = pltpu.SemaphoreType.DMA
    bf16, f32 = jnp.bfloat16, jnp.float32
    blocks = lambda n, kind: pltpu.VMEM((n, members, LANES), kind)
    wide = 3 * lobs + 2 * LANES
    big = nc * nm * ns * wide * 2 > 4 * 2**20
    return pl.pallas_call(
        functools.partial(letkf_kernel, ns, nm, picks),
        in_specs=[smem, smem, smem, hbm, hbm, hbm, hbm, hbm, hbm],
        out_specs=vmem,
        out_shape=pltpu.VMEM(ens.shape, bf16),
        scratch_shapes=[
            pltpu.VMEM(lists.shape, lists.dtype),
            pltpu.VMEM(loc.shape, loc.dtype),
            pltpu.VMEM(loc.shape, f32),
            pltpu.VMEM((CORES, nm, shard, tile_obs), bf16),
            pltpu.VMEM((CORES, his, LANES), bf16),
            pltpu.VMEM((CORES, his, LANES), bf16),
            pltpu.VMEM((CORES, his, LANES), f32),
            pltpu.VMEM((CORES, nc * nm, lobs), lists.dtype),
            pltpu.VMEM((CORES, nc * nm, lobs), f32),
            pltpu.VMEM((CORES, nc * nm, wide), bf16),
            pltpu.VMEM((ns, nc * nm, wide), bf16),
            pltpu.VMEM((nc * ROWS16, 3 * lobs), f32),
            pltpu.VMEM((nc * picks, CORES * his, LANES), f32),
            blocks(nc * picks, f32),
            pltpu.VMEM((nc, picks, members // 2, LANES), f32),
            pltpu.VMEM((nc, picks, members // 2, LANES), f32),
            blocks(picks, f32),
            blocks(picks, f32),
            pltpu.VMEM((picks, members, 1), f32),
            pltpu.VMEM((picks, 1, LANES), f32),
            pltpu.VMEM((slots * members // 2, LANES), bf16),
            pltpu.VMEM((nm, slots * members // 2, LANES), bf16),
            pltpu.VMEM(ens.shape, bf16),
            pltpu.VMEM((oblocks, 1, ens.shape[2]), f32),
            dma((6,)), dma((nm, PARTS)), dma((nm, PARTS)), dma((nm, PARTS)), dma((nm, PARTS)),
            dma((2,)), dma((2,)), dma((ns,)), dma((ns,)), dma((nc,)), dma((nc,)),
            dma((nm,)), dma((nm,)),
        ],
        compiler_params=pltpu.CompilerParams(
            collective_id=0, has_side_effects=True,
            vmem_limit_bytes=56 * 2**20 if big else None,
        ),
        name="analysis",
    )(send, src, frac, lists, loc, pert, prec, innov, ens)


def shards(
    obs_pert,
    innovation,
    obs_prec,
    obs_lists,
    loc_weight,
    send_rows,
    ocean_src,
    ocean_frac,
    ocean_ens,
):
    result = analysis(
        send_rows[0], ocean_src.T, ocean_frac, obs_lists, loc_weight, obs_pert,
        obs_prec.reshape(-1, LANES), innovation.reshape(-1, LANES),
        ocean_ens.transpose(1, 0, 2),
    )
    return result.transpose(1, 0, 2)


def solution(mesh):
    return jax.shard_map(
        shards,
        mesh=mesh,
        in_specs=(
            P("member", "space"),
            P("space"),
            P("space"),
            P("space", None),
            P("space", None),
            P("space", None, None),
            P("space", None),
            P("space"),
            P(None, "space", "member"),
        ),
        out_specs=P(None, "space", "member"),
        check_vma=False,
    )
```

```python
import functools

import jax
import jax.numpy as jnp
from jax import lax
from jax.experimental import pallas as pl
from jax.experimental.pallas import tpu as pltpu
from jax.sharding import PartitionSpec as P

ITERS = 12
LANES = 128
CHUNK = 1024
CORES = 2
ROWS16 = 16
PARTS = 2


def split(value):
    high = value.astype(jnp.bfloat16)
    low = (value - high.astype(jnp.float32)).astype(jnp.bfloat16)
    return high, low


def left_side(value):
    return jnp.concatenate(split(value), axis=1)


def right_side(value):
    pair = left_side(value)
    filler = jnp.zeros((LANES - pair.shape[0], pair.shape[1]), jnp.bfloat16)
    return jnp.concatenate([pair, filler, pair, filler], axis=0)


def halves(product):
    return product[:, :LANES] + product[:, LANES:]


def mm(lhs, rhs):
    return jnp.dot(lhs, rhs, preferred_element_type=jnp.float32)


def xor(value, flip, size):
    result, bit = 0, 1
    while bit < size:
        own = (value // bit) % 2
        result = result + (1 - own if flip & bit else own) * bit
        bit *= 2
    return result


MESH = pl.DeviceIdType.MESH


def remote(src, dst, send_sem, recv_sem, device):
    return pltpu.make_async_remote_copy(
        src_ref=src, dst_ref=dst, send_sem=send_sem, recv_sem=recv_sem,
        device_id=device, device_id_type=MESH,
    )


def letkf_kernel(
    ns, nm, picks,
    send_hbm, src_hbm, frac_hbm, lists_hbm, loc_hbm, pert_ref, prec_ref, innov_ref, ens_hbm, out_ref,
    lists_ref, loc_ref, loc_f32, pert_all, prec_all, innov_all, innov_f32, rows_list, rows_loc,
    message, table, chosen, dense, gram, gram_out, gram_in, root, inverse, pulled, scales, mixed, mixed_in, ens, ens_mean, send_ref, src_ref, frac_ref,
    local_sem, z_send, z_recv, core_send, core_recv, extra_send, extra_recv,
    list_send, list_recv, gram_send, gram_recv, mix_send, mix_recv,
):
    s = lax.axis_index("space")
    m = lax.axis_index("member")
    nc = ns // CORES
    core, chip = s % CORES, s // CORES
    sibling = (s + 1 - 2 * core, m)
    members = pert_ref.shape[0] * nm
    tile_obs = pert_ref.shape[1]
    tile_his = tile_obs // LANES
    part = tile_obs // PARTS
    group_len = lists_ref.shape[0] // nm
    lobs = lists_ref.shape[1]
    oblocks = out_ref.shape[0]
    slots = mixed.shape[0] // (members // 2)
    z_peers = [xor(m, k, nm) for k in range(1, nm)]
    chips = [xor(chip, k, nc) for k in range(1, nc)]
    s_peers = [lax.rem(s + k, ns) for k in range(1, ns)]

    take_lists = pltpu.make_async_copy(lists_hbm, lists_ref, local_sem.at[0])
    take_loc = pltpu.make_async_copy(loc_hbm, loc_ref, local_sem.at[1])
    take_pert = pltpu.make_async_copy(pert_ref, pert_all.at[core, m], local_sem.at[2])
    take_prec = pltpu.make_async_copy(prec_ref, prec_all.at[core], local_sem.at[3])
    take_innov = pltpu.make_async_copy(innov_ref, innov_all.at[core], local_sem.at[4])
    take_ens = pltpu.make_async_copy(ens_hbm, ens, local_sem.at[5])
    take_small = [
        pltpu.make_async_copy(send_hbm, send_ref, local_sem.at[6]),
        pltpu.make_async_copy(src_hbm, src_ref, local_sem.at[7]),
        pltpu.make_async_copy(frac_hbm, frac_ref, local_sem.at[8]),
    ]
    for copy in take_small + [take_lists, take_loc, take_pert, take_prec, take_innov, take_ens]:
        copy.start()

    barrier = pltpu.get_barrier_semaphore()
    for peer in z_peers:
        pl.semaphore_signal(barrier, inc=1, device_id=(s, peer), device_id_type=MESH)
    for peer in s_peers:
        pl.semaphore_signal(barrier, inc=1, device_id=(peer, m), device_id_type=MESH)
    pl.semaphore_wait(barrier, len(z_peers) + len(s_peers))

    def span(h):
        return pl.ds(h * part, part)

    def to_z(peer, h):
        return remote(
            pert_ref.at[:, span(h)], pert_all.at[core, m, :, span(h)],
            z_send.at[peer, h], z_recv.at[m, h], (s, peer),
        )

    def from_z(peer, h):
        return remote(
            pert_ref.at[:, span(h)], pert_all.at[core, peer, :, span(h)],
            z_send.at[m, h], z_recv.at[peer, h], (s, peer),
        )

    def across(owner, h, src):
        return remote(
            src, pert_all.at[core, owner, :, span(h)],
            core_send.at[owner, h], core_recv.at[owner, h], sibling,
        )

    def from_across(owner, h):
        there = pert_all.at[1 - core, owner, :, span(h)]
        return remote(there, there, core_send.at[owner, h], core_recv.at[owner, h], sibling)

    for h in range(PARTS):
        for peer in z_peers:
            to_z(peer, h).start()
    extra_out = [
        remote(prec_ref, prec_all.at[core], extra_send.at[0], extra_recv.at[0], sibling),
        remote(innov_ref, innov_all.at[core], extra_send.at[1], extra_recv.at[1], sibling),
    ]
    extra_in = [
        remote(prec_ref, prec_all.at[1 - core], extra_send.at[0], extra_recv.at[0], sibling),
        remote(innov_ref, innov_all.at[1 - core], extra_send.at[1], extra_recv.at[1], sibling),
    ]
    for copy in extra_out:
        copy.start()
    for h in range(PARTS):
        across(m, h, pert_ref.at[:, span(h)]).start()

    for copy in take_small:
        copy.wait()
    take_lists.wait()
    take_loc.wait()
    loc_f32[...] = loc_ref[...].astype(jnp.float32)
    for parity in range(CORES):
        def pick_rows(t, carry):
            for g in range(nm):
                row = send_ref[g, t * CORES + parity] + g * group_len
                rows_list[parity, pl.ds(t * nm + g, 1), :] = lists_ref[pl.ds(row, 1), :]
                rows_loc[parity, pl.ds(t * nm + g, 1), :] = loc_f32[pl.ds(row, 1), :]
            return carry

        lax.fori_loop(0, nc, pick_rows, 0, unroll=nc <= 4)
        spots = rows_list[parity]
        high = lax.shift_right_logical(spots, 7).astype(jnp.float32)
        low = jnp.bitwise_and(spots, LANES - 1).astype(jnp.float32)
        message[parity, :, 0:lobs] = high.astype(jnp.bfloat16)
        message[parity, :, lobs : 2 * lobs] = low.astype(jnp.bfloat16)
        message[parity, :, 2 * lobs : 3 * lobs] = rows_loc[parity].astype(jnp.bfloat16)
    pick_row = lax.broadcasted_iota(jnp.int32, (table.shape[1], LANES), 0)
    tile_of = jnp.zeros((table.shape[1], LANES), jnp.int32)
    group_of = jnp.zeros((table.shape[1], LANES), jnp.int32)
    for p in range(picks):
        q = m * picks + p
        slot = src_ref[q % 2, q // 2]
        tile_of = jnp.where(pick_row == p, slot % ns, tile_of)
        group_of = jnp.where(pick_row == p, slot // ns, group_of)
    for parity in range(CORES):
        message[parity, :, 3 * lobs : 3 * lobs + LANES] = (
            tile_of.astype(jnp.float32).astype(jnp.bfloat16)
        )
        message[parity, :, 3 * lobs + LANES :] = group_of.astype(jnp.float32).astype(jnp.bfloat16)

    def list_to(peer):
        return remote(
            message.at[peer % CORES], table.at[s], list_send.at[peer], list_recv.at[s], (peer, m)
        )

    def list_from(peer):
        return remote(
            message.at[core], table.at[peer], list_send.at[peer], list_recv.at[peer], (peer, m)
        )

    for peer in s_peers:
        list_to(peer).start()
    table[s] = message[core]
    gram[...] = jnp.zeros_like(gram)
    for peer in s_peers:
        list_from(peer).wait_recv()

    deep = nc * ROWS16
    per_tile = table.shape[1]
    tiles_col, rows_col = [], []
    for t in range(nc):
        cut = table[t * CORES + core, 0:ROWS16, 3 * lobs :].astype(jnp.float32)
        tiles_col.append(cut[:, 0:1])
        rows_col.append(cut[:, LANES : LANES + 1] + float(t * nm))
    tiles_col = jnp.concatenate(tiles_col, axis=0).astype(jnp.int32)
    rows_col = jnp.concatenate(rows_col, axis=0).astype(jnp.int32)
    at_row = lax.broadcasted_iota(jnp.int32, (deep, per_tile), 1) == rows_col

    def select(t):
        hot = jnp.where(jnp.logical_and(at_row, tiles_col == t), 1.0, 0.0).astype(jnp.bfloat16)
        return mm(hot, table[t, :, 0 : 3 * lobs])

    if ns <= 8:
        total = select(0)
        for t in range(1, ns):
            total += select(t)
        chosen[...] = total
    else:
        chosen[...] = jnp.zeros_like(chosen)

        def select_step(t, carry):
            chosen[...] += select(t)
            return carry

        lax.fori_loop(0, ns, select_step, 0)
    shift = (tiles_col - 1) * tile_his - chip * (CORES * tile_his)
    spots = chosen[:, 0:lobs] + shift.astype(jnp.float32)
    around = float(ns * tile_his)
    spots = jnp.where(spots < 0.0, spots + around, spots)
    chosen[:, 0:lobs] = jnp.where(spots >= around, spots - around, spots)

    for copy in (take_prec, take_innov):
        copy.wait()
    for copy in extra_in:
        copy.wait_recv()
    innov_f32[...] = innov_all[...].astype(jnp.float32)
    his = CORES * tile_his
    hi_iota = lax.broadcasted_iota(jnp.int32, (his, lobs), 0).astype(jnp.float32)
    lo_iota = lax.broadcasted_iota(jnp.int32, (LANES, lobs), 0).astype(jnp.float32)
    prec = jnp.concatenate([prec_all[i].astype(jnp.float32) for i in range(CORES)], axis=0)
    contract = (((1,), (1,)), ((), ()))

    def spread(t, carry):
        for p in range(picks):
            row = pl.ds(t * ROWS16 + p, 1)
            high, low = chosen[row, 0:lobs], chosen[row, lobs : 2 * lobs]
            taper = chosen[row, 2 * lobs : 3 * lobs]
            hi_hot = jnp.where(hi_iota == high, taper, 0.0).astype(jnp.bfloat16)
            lo_hot = jnp.where(lo_iota == low, 1.0, 0.0).astype(jnp.bfloat16)
            dense[t * picks + p] = prec * lax.dot_general(
                hi_hot, lo_hot, contract, preferred_element_type=jnp.float32
            )
        return carry

    lax.fori_loop(0, nc, spread, 0)

    per = CHUNK // LANES

    def take_chunk(tile, first):
        where = pl.ds(pl.multiple_of(first, CHUNK), CHUNK)
        wide = jnp.concatenate(
            [pert_all[tile, i, :, where].astype(jnp.float32) for i in range(nm)], axis=0
        )
        line = jnp.concatenate(
            [innov_f32[tile, pl.ds(first // LANES + j, 1), :] for j in range(per)], axis=1
        )
        line = jnp.where(lax.broadcasted_iota(jnp.int32, (ROWS16, CHUNK), 0) == 0, line, 0.0)
        return wide, jnp.concatenate([wide, line], axis=0).astype(jnp.bfloat16)

    def add_tile(t, tile, first, wide, cells):
        for p in range(picks):
            b = t * picks + p
            parts = []
            for j in range(per):
                at = pl.ds(tile * tile_his + first // LANES + j, 1)
                parts.append(wide[:, j * LANES : (j + 1) * LANES] * dense[b, at, :])
            high, low = split(jnp.concatenate(parts, axis=1))
            gram[b, :, : cells.shape[0]] += lax.dot_general(
                high, cells, contract, preferred_element_type=jnp.float32
            ) + lax.dot_general(low, cells, contract, preferred_element_type=jnp.float32)

    def add_part(tile, h):
        def chunk_step(c, carry):
            first = h * part + c * CHUNK
            wide, cells = take_chunk(tile, first)

            def pick_step(t, carry):
                add_tile(t, tile, first, wide, cells)
                return carry

            lax.fori_loop(0, nc, pick_step, 0, unroll=nc <= 4)
            return carry

        lax.fori_loop(0, part // CHUNK, chunk_step, 0)

    half = members // 2
    turn = half + 1
    low_cols = lax.broadcasted_iota(jnp.int32, (half, LANES), 1)

    def pack(t):
        for p in range(picks):
            b = t * picks + p
            under = jnp.where(low_cols >= half, gram[b, half:, :], 0.0)
            gram_out[t, p] = gram[b, :half, :] + pltpu.roll(under, turn, 1)

    def arrive(h):
        for peer in z_peers:
            from_z(peer, h).wait_recv()
            across(peer, h, pert_all.at[core, peer, :, span(h)]).start()

    def arrive_across(h):
        for i in range(nm):
            from_across(i, h).wait_recv()

    def gram_to(peer):
        return remote(
            gram_out.at[peer], gram_in.at[chip],
            gram_send.at[peer], gram_recv.at[chip], (peer * CORES + core, m),
        )

    def gram_from(peer):
        return remote(
            gram_out.at[peer], gram_in.at[peer],
            gram_send.at[peer], gram_recv.at[peer], (peer * CORES + core, m),
        )

    take_ens.wait()

    def center(o, carry):
        wide = ens[o].astype(jnp.float32)
        mean = jnp.sum(wide, axis=0, keepdims=True) * (1.0 / members)
        ens_mean[o] = mean
        ens[o] = (wide - mean).astype(jnp.bfloat16)
        return carry

    lax.fori_loop(0, oblocks, center, 0)
    take_pert.wait()
    for h in range(PARTS):
        arrive(h)
        add_part(core, h)
        arrive_across(h)
        if h + 1 < PARTS or nc > 4 or part > CHUNK:
            add_part(1 - core, h)

    if nc <= 4 and part <= CHUNK:
        first = (PARTS - 1) * part
        wide, cells = take_chunk(1 - core, first)
        for t in chips[::-1] + [chip]:
            add_tile(t, 1 - core, first, wide, cells)
            pack(t)
            if t is not chip:
                gram_to(t).start()
    else:

        def pack_step(t, carry):
            pack(t)
            return carry

        lax.fori_loop(0, nc, pack_step, 0)
        for peer in reversed(chips):
            gram_to(peer).start()

    rows = lax.broadcasted_iota(jnp.int32, (members, LANES), 0)
    cols = lax.broadcasted_iota(jnp.int32, (members, LANES), 1)
    on_diag = rows == cols
    half3 = jnp.where(on_diag, 1.5, 0.0)

    for peer in chips:
        gram_from(peer).wait_recv()
    filler = jnp.zeros((LANES - half, LANES), jnp.float32)
    for p in range(picks):
        top = gram_out[chip, p]
        for peer in chips:
            top += gram_in[peer, p]
        under = pltpu.roll(top, LANES - turn, 1)
        flipped = jnp.concatenate([top, filler], axis=0).T[half : 2 * half]
        both = jnp.concatenate([top, jnp.where(low_cols < half, flipped, under)], axis=0)
        pulled[p] = jnp.sum(jnp.where(cols == members, both, 0.0), axis=1, keepdims=True)
        matrix = jnp.where(cols < members, both, 0.0) + jnp.where(on_diag, members - 1.0, 0.0)
        scale = jnp.sum(
            jnp.sum(jnp.where(on_diag, matrix, 0.0), axis=1, keepdims=True), axis=0, keepdims=True
        )
        scales[p] = jnp.broadcast_to(scale, (1, LANES))
        start = matrix / scale
        correction = half3 - 0.5 * start
        root[p] = halves(mm(left_side(start), right_side(correction)))
        inverse[p] = correction

    def newton(step, carry):
        corrections, pairs = [], []
        space = jnp.zeros((LANES - members, 2 * LANES), jnp.bfloat16)
        for p in range(picks):
            r, z = left_side(root[p]), left_side(inverse[p])
            rhs = jnp.concatenate([r, space, r, space], axis=0)
            corrections.append(half3 - 0.5 * halves(mm(z, rhs)))
            pairs.append(jnp.concatenate([r, z], axis=0))
        for p in range(picks):
            both = halves(mm(pairs[p], right_side(corrections[p])))
            root[p] = both[:members]
            inverse[p] = both[members:]
        return carry

    lax.fori_loop(0, ITERS - 1, newton, 0, unroll=picks <= 4)

    sums = [jnp.zeros((members, LANES), jnp.float32) for _ in range(slots)]
    means = [jnp.zeros((members, 1), jnp.float32) for _ in range(slots)]
    base = (m * picks) // 2
    for p in range(picks):
        z = inverse[p]
        scale = scales[p]
        half_way = jnp.sum(z * pulled[p], axis=0, keepdims=True)
        mean_weight = jnp.sum(z * half_way, axis=1, keepdims=True) / scale[:, :1]
        trans = jnp.sqrt((members - 1.0) / scale) * z
        q = m * picks + p
        o = q // 2
        frac = frac_ref[o]
        weight = jnp.where(q % 2 == 0, 1.0 - frac, frac)
        for j in range(max(0, p // 2), min(slots, p // 2 + 2)):
            share = jnp.where(o - base == j, weight, 0.0)
            sums[j] += share * trans
            means[j] += share * mean_weight
    for j in range(slots):
        under = jnp.where(low_cols < half, 0.0, jnp.where(low_cols < members, sums[j][half:], 0.0))
        packed = sums[j][:half] + pltpu.roll(under, half, 1)
        high = means[j].astype(jnp.bfloat16).astype(jnp.float32)
        tails = (high, means[j] - high)
        for k in range(4):
            tail = tails[k // 2][(k % 2) * half : (k % 2 + 1) * half]
            packed = jnp.where(low_cols == members + half + k, tail, packed)
        mixed[j * half : (j + 1) * half, :] = packed.astype(jnp.bfloat16)

    def mix_to(peer):
        return remote(mixed, mixed_in.at[m], mix_send.at[peer], mix_recv.at[m], (s, peer))

    def mix_from(peer):
        return remote(mixed, mixed_in.at[peer], mix_send.at[peer], mix_recv.at[peer], (s, peer))

    for peer in z_peers:
        mix_to(peer).start()
    mixed_in[m] = mixed[...]
    for peer in chips:
        gram_to(peer).wait_send()
    for peer in s_peers:
        list_to(peer).wait_send()
    for copy in extra_out:
        copy.wait_send()
    for h in range(PARTS):
        for peer in z_peers:
            to_z(peer, h).wait_send()
            across(peer, h, pert_all.at[core, peer, :, span(h)]).wait_send()
        across(m, h, pert_ref.at[:, span(h)]).wait_send()
    for peer in z_peers:
        mix_from(peer).wait_recv()
    def finish(o, owner, j):
        total = mixed_in[owner, j * half : (j + 1) * half].astype(jnp.float32)
        if picks % 2 and j == slots - 1 and owner % 2 == 0:
            total += mixed_in[owner + 1, 0:half].astype(jnp.float32)
        flipped = jnp.concatenate([total, filler], axis=0).T[half : 2 * half]
        under = jnp.where(low_cols < half, flipped, pltpu.roll(total, LANES - half, 1))
        first = members + half
        tail = total[:, first : first + 2] + total[:, first + 2 : first + 4]
        tail = jnp.concatenate([tail[:, 0:1], tail[:, 1:2]], axis=0)
        line = jnp.sum(jnp.where(on_diag, tail, 0.0), axis=0, keepdims=True)
        weights = jnp.concatenate([total, under], axis=0) + line
        weights = weights.astype(jnp.bfloat16)[:, :members]
        out_ref[o] = (ens_mean[o] + mm(weights, ens[o])).astype(jnp.bfloat16)

    if oblocks <= 8:
        for o in range(oblocks):
            owner = (2 * o) // picks
            finish(o, owner, o - (owner * picks) // 2)
    else:

        def finish_step(owner, carry):
            for j in range(slots):
                finish(owner * slots + j, owner, j)
            return carry

        lax.fori_loop(0, nm, finish_step, 0)
    for peer in z_peers:
        mix_to(peer).wait_send()


def analysis(send, src, frac, lists, loc, pert, prec, innov, ens):
    ns, nm = lax.axis_size("space"), lax.axis_size("member")
    shard, tile_obs = pert.shape
    members = shard * nm
    oblocks = src.shape[1]
    nc = ns // CORES
    picks = 2 * oblocks // nm
    assert picks * nm == 2 * oblocks and picks <= ROWS16
    assert picks % 2 == 0 or oblocks <= 8
    slots = picks // 2 + picks % 2
    his = tile_obs // LANES
    lobs = lists.shape[1]
    vmem = pl.BlockSpec(memory_space=pltpu.VMEM)
    hbm = pl.BlockSpec(memory_space=pl.ANY)
    dma = pltpu.SemaphoreType.DMA
    bf16, f32 = jnp.bfloat16, jnp.float32
    blocks = lambda n, kind: pltpu.VMEM((n, members, LANES), kind)
    wide = 3 * lobs + 2 * LANES
    big = nc * nm * ns * wide * 2 > 4 * 2**20
    return pl.pallas_call(
        functools.partial(letkf_kernel, ns, nm, picks),
        in_specs=[hbm, hbm, hbm, hbm, hbm, hbm, hbm, hbm, hbm],
        out_specs=vmem,
        out_shape=pltpu.VMEM(ens.shape, bf16),
        scratch_shapes=[
            pltpu.VMEM(lists.shape, lists.dtype),
            pltpu.VMEM(loc.shape, loc.dtype),
            pltpu.VMEM(loc.shape, f32),
            pltpu.VMEM((CORES, nm, shard, tile_obs), bf16),
            pltpu.VMEM((CORES, his, LANES), bf16),
            pltpu.VMEM((CORES, his, LANES), bf16),
            pltpu.VMEM((CORES, his, LANES), f32),
            pltpu.VMEM((CORES, nc * nm, lobs), lists.dtype),
            pltpu.VMEM((CORES, nc * nm, lobs), f32),
            pltpu.VMEM((CORES, nc * nm, wide), bf16),
            pltpu.VMEM((ns, nc * nm, wide), bf16),
            pltpu.VMEM((nc * ROWS16, 3 * lobs), f32),
            pltpu.VMEM((nc * picks, CORES * his, LANES), f32),
            blocks(nc * picks, f32),
            pltpu.VMEM((nc, picks, members // 2, LANES), f32),
            pltpu.VMEM((nc, picks, members // 2, LANES), f32),
            blocks(picks, f32),
            blocks(picks, f32),
            pltpu.VMEM((picks, members, 1), f32),
            pltpu.VMEM((picks, 1, LANES), f32),
            pltpu.VMEM((slots * members // 2, LANES), bf16),
            pltpu.VMEM((nm, slots * members // 2, LANES), bf16),
            pltpu.VMEM(ens.shape, bf16),
            pltpu.VMEM((oblocks, 1, ens.shape[2]), f32),
            pltpu.SMEM(send.shape, send.dtype),
            pltpu.SMEM(src.shape, src.dtype),
            pltpu.SMEM(frac.shape, frac.dtype),
            dma((9,)), dma((nm, PARTS)), dma((nm, PARTS)), dma((nm, PARTS)), dma((nm, PARTS)),
            dma((2,)), dma((2,)), dma((ns,)), dma((ns,)), dma((nc,)), dma((nc,)),
            dma((nm,)), dma((nm,)),
        ],
        compiler_params=pltpu.CompilerParams(
            collective_id=0, has_side_effects=True,
            vmem_limit_bytes=56 * 2**20 if big else None,
        ),
        name="analysis",
    )(send, src, frac, lists, loc, pert, prec, innov, ens)


def shards(
    obs_pert,
    innovation,
    obs_prec,
    obs_lists,
    loc_weight,
    send_rows,
    ocean_src,
    ocean_frac,
    ocean_ens,
):
    result = analysis(
        send_rows[0], ocean_src.T, ocean_frac, obs_lists, loc_weight, obs_pert,
        obs_prec.reshape(-1, LANES), innovation.reshape(-1, LANES),
        ocean_ens.transpose(1, 0, 2),
    )
    return result.transpose(1, 0, 2)


def solution(mesh):
    return jax.shard_map(
        shards,
        mesh=mesh,
        in_specs=(
            P("member", "space"),
            P("space"),
            P("space"),
            P("space", None),
            P("space", None),
            P("space", None, None),
            P("space", None),
            P("space"),
            P(None, "space", "member"),
        ),
        out_specs=P(None, "space", "member"),
        check_vma=False,
    )
```

```python
import functools

import jax
import jax.numpy as jnp
from jax import lax
from jax.experimental import pallas as pl
from jax.experimental.pallas import tpu as pltpu
from jax.sharding import PartitionSpec as P

ITERS = 12
LANES = 128
CORES = 2
ROWS16 = 16
PARTS = 2


def split(value):
    high = value.astype(jnp.bfloat16)
    low = (value - high.astype(jnp.float32)).astype(jnp.bfloat16)
    return high, low


def left_side(value):
    return jnp.concatenate(split(value), axis=1)


def right_side(value):
    pair = left_side(value)
    filler = jnp.zeros((LANES - pair.shape[0], pair.shape[1]), jnp.bfloat16)
    return jnp.concatenate([pair, filler, pair, filler], axis=0)


def halves(product):
    return product[:, :LANES] + product[:, LANES:]


def mm(lhs, rhs):
    return jnp.dot(lhs, rhs, preferred_element_type=jnp.float32)


def xor(value, flip, size):
    result, bit = 0, 1
    while bit < size:
        own = (value // bit) % 2
        result = result + (1 - own if flip & bit else own) * bit
        bit *= 2
    return result


MESH = pl.DeviceIdType.MESH


def remote(src, dst, send_sem, recv_sem, device):
    return pltpu.make_async_remote_copy(
        src_ref=src, dst_ref=dst, send_sem=send_sem, recv_sem=recv_sem,
        device_id=device, device_id_type=MESH,
    )


def letkf_kernel(
    ns, nm, picks,
    send_hbm, src_hbm, frac_hbm, lists_hbm, loc_hbm, pert_ref, prec_ref, innov_ref, ens_hbm, out_ref,
    lists_ref, loc_ref, loc_f32, pert_all, prec_all, innov_all, innov_f32, rows_list, rows_loc,
    message, table, chosen, dense, gram, gram_out, gram_in, root, inverse, pulled, scales, mixed, mixed_in, ens, ens_mean, send_ref, src_ref, frac_ref,
    local_sem, z_send, z_recv, core_send, core_recv, extra_send, extra_recv,
    list_send, list_recv, gram_send, gram_recv, mix_send, mix_recv,
):
    s = lax.axis_index("space")
    m = lax.axis_index("member")
    nc = ns // CORES
    core, chip = s % CORES, s // CORES
    sibling = (s + 1 - 2 * core, m)
    members = pert_ref.shape[0] * nm
    tile_obs = pert_ref.shape[1]
    tile_his = tile_obs // LANES
    cut = tile_his * 6 // 16 * LANES
    bounds = [(0, cut), (cut, tile_obs - cut)]
    group_len = lists_ref.shape[0] // nm
    lobs = lists_ref.shape[1]
    oblocks = out_ref.shape[0]
    slots = mixed.shape[0] // (members // 2)
    z_peers = [xor(m, k, nm) for k in range(1, nm)]
    chips = [xor(chip, k, nc) for k in range(1, nc)]
    s_peers = [lax.rem(s + k, ns) for k in range(1, ns)]

    barrier = pltpu.get_barrier_semaphore()
    for peer in z_peers:
        pl.semaphore_signal(barrier, inc=1, device_id=(s, peer), device_id_type=MESH)
    for peer in s_peers:
        pl.semaphore_signal(barrier, inc=1, device_id=(peer, m), device_id_type=MESH)

    take_lists = pltpu.make_async_copy(lists_hbm, lists_ref, local_sem.at[0])
    take_loc = pltpu.make_async_copy(loc_hbm, loc_ref, local_sem.at[1])
    take_pert = pltpu.make_async_copy(pert_ref, pert_all.at[core, m], local_sem.at[2])
    take_prec = pltpu.make_async_copy(prec_ref, prec_all.at[core], local_sem.at[3])
    take_innov = pltpu.make_async_copy(innov_ref, innov_all.at[core], local_sem.at[4])
    take_ens = pltpu.make_async_copy(ens_hbm, ens, local_sem.at[5])
    take_small = [
        pltpu.make_async_copy(send_hbm, send_ref, local_sem.at[6]),
        pltpu.make_async_copy(src_hbm, src_ref, local_sem.at[7]),
        pltpu.make_async_copy(frac_hbm, frac_ref, local_sem.at[8]),
    ]
    for copy in take_small + [take_lists, take_loc, take_pert, take_prec, take_innov, take_ens]:
        copy.start()

    pl.semaphore_wait(barrier, len(z_peers) + len(s_peers))

    def span(h):
        return pl.ds(*bounds[h])

    def to_z(peer, h):
        return remote(
            pert_ref.at[:, span(h)], pert_all.at[core, m, :, span(h)],
            z_send.at[peer, h], z_recv.at[m, h], (s, peer),
        )

    def from_z(peer, h):
        return remote(
            pert_ref.at[:, span(h)], pert_all.at[core, peer, :, span(h)],
            z_send.at[m, h], z_recv.at[peer, h], (s, peer),
        )

    def across(owner, h, src):
        return remote(
            src, pert_all.at[core, owner, :, span(h)],
            core_send.at[owner, h], core_recv.at[owner, h], sibling,
        )

    def from_across(owner, h):
        there = pert_all.at[1 - core, owner, :, span(h)]
        return remote(there, there, core_send.at[owner, h], core_recv.at[owner, h], sibling)

    for h in range(PARTS):
        for peer in z_peers:
            to_z(peer, h).start()
    extra_out = [
        remote(prec_ref, prec_all.at[core], extra_send.at[0], extra_recv.at[0], sibling),
        remote(innov_ref, innov_all.at[core], extra_send.at[1], extra_recv.at[1], sibling),
    ]
    extra_in = [
        remote(prec_ref, prec_all.at[1 - core], extra_send.at[0], extra_recv.at[0], sibling),
        remote(innov_ref, innov_all.at[1 - core], extra_send.at[1], extra_recv.at[1], sibling),
    ]
    for copy in extra_out:
        copy.start()
    for h in range(PARTS):
        across(m, h, pert_ref.at[:, span(h)]).start()

    for copy in take_small:
        copy.wait()
    take_lists.wait()
    take_loc.wait()
    loc_f32[...] = loc_ref[...].astype(jnp.float32)
    for parity in range(CORES):
        def pick_rows(t, carry):
            for g in range(nm):
                row = send_ref[g, t * CORES + parity] + g * group_len
                rows_list[parity, pl.ds(t * nm + g, 1), :] = lists_ref[pl.ds(row, 1), :]
                rows_loc[parity, pl.ds(t * nm + g, 1), :] = loc_f32[pl.ds(row, 1), :]
            return carry

        lax.fori_loop(0, nc, pick_rows, 0, unroll=nc <= 4)
        spots = rows_list[parity]
        high = lax.shift_right_logical(spots, 7).astype(jnp.float32)
        low = jnp.bitwise_and(spots, LANES - 1).astype(jnp.float32)
        message[parity, :, 0:lobs] = high.astype(jnp.bfloat16)
        message[parity, :, lobs : 2 * lobs] = low.astype(jnp.bfloat16)
        message[parity, :, 2 * lobs : 3 * lobs] = rows_loc[parity].astype(jnp.bfloat16)
    pick_row = lax.broadcasted_iota(jnp.int32, (table.shape[1], LANES), 0)
    tile_of = jnp.zeros((table.shape[1], LANES), jnp.int32)
    group_of = jnp.zeros((table.shape[1], LANES), jnp.int32)
    for p in range(picks):
        q = m * picks + p
        slot = src_ref[q % 2, q // 2]
        tile_of = jnp.where(pick_row == p, slot % ns, tile_of)
        group_of = jnp.where(pick_row == p, slot // ns, group_of)
    for parity in range(CORES):
        message[parity, :, 3 * lobs : 3 * lobs + LANES] = (
            tile_of.astype(jnp.float32).astype(jnp.bfloat16)
        )
        message[parity, :, 3 * lobs + LANES :] = group_of.astype(jnp.float32).astype(jnp.bfloat16)

    def list_to(peer):
        return remote(
            message.at[peer % CORES], table.at[s], list_send.at[peer], list_recv.at[s], (peer, m)
        )

    def list_from(peer):
        return remote(
            message.at[core], table.at[peer], list_send.at[peer], list_recv.at[peer], (peer, m)
        )

    for peer in s_peers:
        list_to(peer).start()
    table[s] = message[core]
    gram[...] = jnp.zeros_like(gram)
    for peer in s_peers:
        list_from(peer).wait_recv()

    deep = nc * ROWS16
    per_tile = table.shape[1]
    tiles_col, rows_col = [], []
    for t in range(nc):
        cut = table[t * CORES + core, 0:ROWS16, 3 * lobs :].astype(jnp.float32)
        tiles_col.append(cut[:, 0:1])
        rows_col.append(cut[:, LANES : LANES + 1] + float(t * nm))
    tiles_col = jnp.concatenate(tiles_col, axis=0).astype(jnp.int32)
    rows_col = jnp.concatenate(rows_col, axis=0).astype(jnp.int32)
    at_row = lax.broadcasted_iota(jnp.int32, (deep, per_tile), 1) == rows_col

    def select(t):
        hot = jnp.where(jnp.logical_and(at_row, tiles_col == t), 1.0, 0.0).astype(jnp.bfloat16)
        return mm(hot, table[t, :, 0 : 3 * lobs])

    if ns <= 8:
        total = select(0)
        for t in range(1, ns):
            total += select(t)
        chosen[...] = total
    else:
        chosen[...] = jnp.zeros_like(chosen)

        def select_step(t, carry):
            chosen[...] += select(t)
            return carry

        lax.fori_loop(0, ns, select_step, 0)
    shift = (tiles_col - 1) * tile_his - chip * (CORES * tile_his)
    spots = chosen[:, 0:lobs] + shift.astype(jnp.float32)
    around = float(ns * tile_his)
    spots = jnp.where(spots < 0.0, spots + around, spots)
    chosen[:, 0:lobs] = jnp.where(spots >= around, spots - around, spots)

    for copy in (take_prec, take_innov):
        copy.wait()
    for copy in extra_in:
        copy.wait_recv()
    innov_f32[...] = innov_all[...].astype(jnp.float32)
    his = CORES * tile_his
    hi_iota = lax.broadcasted_iota(jnp.int32, (his, lobs), 0).astype(jnp.float32)
    lo_iota = lax.broadcasted_iota(jnp.int32, (LANES, lobs), 0).astype(jnp.float32)
    prec = jnp.concatenate([prec_all[i].astype(jnp.float32) for i in range(CORES)], axis=0)
    contract = (((1,), (1,)), ((), ()))

    def spread(t, carry):
        for p in range(picks):
            row = pl.ds(t * ROWS16 + p, 1)
            high, low = chosen[row, 0:lobs], chosen[row, lobs : 2 * lobs]
            taper = chosen[row, 2 * lobs : 3 * lobs]
            hi_hot = jnp.where(hi_iota == high, taper, 0.0).astype(jnp.bfloat16)
            lo_hot = jnp.where(lo_iota == low, 1.0, 0.0).astype(jnp.bfloat16)
            dense[t * picks + p] = prec * lax.dot_general(
                hi_hot, lo_hot, contract, preferred_element_type=jnp.float32
            )
        return carry

    lax.fori_loop(0, nc, spread, 0)

    def take_chunk(tile, h):
        wide = jnp.concatenate(
            [pert_all[tile, i, :, span(h)].astype(jnp.float32) for i in range(nm)], axis=0
        )
        first, count = bounds[h]
        line = jnp.concatenate(
            [
                innov_f32[tile, pl.ds(first // LANES + j, 1), :]
                for j in range(count // LANES)
            ],
            axis=1,
        )
        line = jnp.where(lax.broadcasted_iota(jnp.int32, (ROWS16, count), 0) == 0, line, 0.0)
        return wide, jnp.concatenate([wide, line], axis=0).astype(jnp.bfloat16)

    def add_tile(t, tile, h, wide, cells):
        first = bounds[h][0]
        per = bounds[h][1] // LANES
        for p in range(picks):
            b = t * picks + p
            parts = []
            for j in range(per):
                at = pl.ds(tile * tile_his + first // LANES + j, 1)
                parts.append(wide[:, j * LANES : (j + 1) * LANES] * dense[b, at, :])
            high, low = split(jnp.concatenate(parts, axis=1))
            gram[b, :, : cells.shape[0]] += lax.dot_general(
                high, cells, contract, preferred_element_type=jnp.float32
            ) + lax.dot_general(low, cells, contract, preferred_element_type=jnp.float32)

    def add_part(tile, h):
        wide, cells = take_chunk(tile, h)

        def pick_step(t, carry):
            add_tile(t, tile, h, wide, cells)
            return carry

        lax.fori_loop(0, nc, pick_step, 0, unroll=nc <= 4)

    half = members // 2
    turn = half + 1
    low_cols = lax.broadcasted_iota(jnp.int32, (half, LANES), 1)

    def pack(t):
        for p in range(picks):
            b = t * picks + p
            under = jnp.where(low_cols >= half, gram[b, half:, :], 0.0)
            gram_out[t, p] = gram[b, :half, :] + pltpu.roll(under, turn, 1)

    def arrive(h):
        for peer in z_peers:
            from_z(peer, h).wait_recv()
            across(peer, h, pert_all.at[core, peer, :, span(h)]).start()

    def arrive_across(h):
        for i in range(nm):
            from_across(i, h).wait_recv()

    def gram_to(peer):
        return remote(
            gram_out.at[peer], gram_in.at[chip],
            gram_send.at[peer], gram_recv.at[chip], (peer * CORES + core, m),
        )

    def gram_from(peer):
        return remote(
            gram_out.at[peer], gram_in.at[peer],
            gram_send.at[peer], gram_recv.at[peer], (peer * CORES + core, m),
        )

    take_pert.wait()
    for h in range(PARTS):
        arrive(h)
        add_part(core, h)
        arrive_across(h)
        if h + 1 < PARTS or nc > 4:
            add_part(1 - core, h)

    if nc <= 4:
        wide, cells = take_chunk(1 - core, PARTS - 1)
        for t in chips[::-1] + [chip]:
            add_tile(t, 1 - core, PARTS - 1, wide, cells)
            pack(t)
            if t is not chip:
                gram_to(t).start()
    else:

        def pack_step(t, carry):
            pack(t)
            return carry

        lax.fori_loop(0, nc, pack_step, 0)
        for peer in reversed(chips):
            gram_to(peer).start()

    take_ens.wait()

    def center(o, carry):
        wide = ens[o].astype(jnp.float32)
        mean = jnp.sum(wide, axis=0, keepdims=True) * (1.0 / members)
        ens_mean[o] = mean
        ens[o] = (wide - mean).astype(jnp.bfloat16)
        return carry

    lax.fori_loop(0, oblocks, center, 0)

    rows = lax.broadcasted_iota(jnp.int32, (members, LANES), 0)
    cols = lax.broadcasted_iota(jnp.int32, (members, LANES), 1)
    on_diag = rows == cols
    half3 = jnp.where(on_diag, 1.5, 0.0)

    for peer in chips:
        gram_from(peer).wait_recv()
    filler = jnp.zeros((LANES - half, LANES), jnp.float32)
    for p in range(picks):
        top = gram_out[chip, p]
        for peer in chips:
            top += gram_in[peer, p]
        under = pltpu.roll(top, LANES - turn, 1)
        flipped = jnp.concatenate([top, filler], axis=0).T[half : 2 * half]
        both = jnp.concatenate([top, jnp.where(low_cols < half, flipped, under)], axis=0)
        pulled[p] = jnp.sum(jnp.where(cols == members, both, 0.0), axis=1, keepdims=True)
        matrix = jnp.where(cols < members, both, 0.0) + jnp.where(on_diag, members - 1.0, 0.0)
        scale = jnp.sum(
            jnp.sum(jnp.where(on_diag, matrix, 0.0), axis=1, keepdims=True), axis=0, keepdims=True
        )
        scales[p] = jnp.broadcast_to(scale, (1, LANES))
        start = matrix / scale
        correction = half3 - 0.5 * start
        root[p] = halves(mm(left_side(start), right_side(correction)))
        inverse[p] = correction

    def newton(step, carry, last=False):
        corrections, pairs = [], []
        space = jnp.zeros((LANES - members, 2 * LANES), jnp.bfloat16)
        for p in range(picks):
            r, z = left_side(root[p]), left_side(inverse[p])
            rhs = jnp.concatenate([r, space, r, space], axis=0)
            corrections.append(half3 - 0.5 * halves(mm(z, rhs)))
            pairs.append(z if last else jnp.concatenate([r, z], axis=0))
        for p in range(picks):
            both = halves(mm(pairs[p], right_side(corrections[p])))
            if not last:
                root[p] = both[:members]
            inverse[p] = both[-members:]
        return carry

    lax.fori_loop(0, ITERS - 2, newton, 0, unroll=picks <= 4)
    newton(ITERS - 2, 0, last=True)

    sums = [jnp.zeros((members, LANES), jnp.float32) for _ in range(slots)]
    means = [jnp.zeros((members, 1), jnp.float32) for _ in range(slots)]
    base = (m * picks) // 2
    for p in range(picks):
        z = inverse[p]
        scale = scales[p]
        half_way = jnp.sum(z * pulled[p], axis=0, keepdims=True)
        mean_weight = jnp.sum(z * half_way, axis=1, keepdims=True) / scale[:, :1]
        trans = jnp.sqrt((members - 1.0) / scale) * z
        q = m * picks + p
        o = q // 2
        frac = frac_ref[o]
        weight = jnp.where(q % 2 == 0, 1.0 - frac, frac)
        for j in range(max(0, p // 2), min(slots, p // 2 + 2)):
            share = jnp.where(o - base == j, weight, 0.0)
            sums[j] += share * trans
            means[j] += share * mean_weight
    for j in range(slots):
        under = jnp.where(low_cols < half, 0.0, jnp.where(low_cols < members, sums[j][half:], 0.0))
        packed = sums[j][:half] + pltpu.roll(under, half, 1)
        high = means[j].astype(jnp.bfloat16).astype(jnp.float32)
        tails = (high, means[j] - high)
        for k in range(4):
            tail = tails[k // 2][(k % 2) * half : (k % 2 + 1) * half]
            packed = jnp.where(low_cols == members + half + k, tail, packed)
        mixed[j * half : (j + 1) * half, :] = packed.astype(jnp.bfloat16)

    def mix_to(peer):
        return remote(mixed, mixed_in.at[m], mix_send.at[peer], mix_recv.at[m], (s, peer))

    def mix_from(peer):
        return remote(mixed, mixed_in.at[peer], mix_send.at[peer], mix_recv.at[peer], (s, peer))

    for peer in z_peers:
        mix_to(peer).start()
    mixed_in[m] = mixed[...]
    for peer in chips:
        gram_to(peer).wait_send()
    for peer in s_peers:
        list_to(peer).wait_send()
    for copy in extra_out:
        copy.wait_send()
    for h in range(PARTS):
        for peer in z_peers:
            to_z(peer, h).wait_send()
            across(peer, h, pert_all.at[core, peer, :, span(h)]).wait_send()
        across(m, h, pert_ref.at[:, span(h)]).wait_send()
    for peer in z_peers:
        mix_from(peer).wait_recv()
    def finish(o, owner, j):
        total = mixed_in[owner, j * half : (j + 1) * half].astype(jnp.float32)
        if picks % 2 and j == slots - 1 and owner % 2 == 0:
            total += mixed_in[owner + 1, 0:half].astype(jnp.float32)
        flipped = jnp.concatenate([total, filler], axis=0).T[half : 2 * half]
        under = jnp.where(low_cols < half, flipped, pltpu.roll(total, LANES - half, 1))
        first = members + half
        tail = total[:, first : first + 2] + total[:, first + 2 : first + 4]
        tail = jnp.concatenate([tail[:, 0:1], tail[:, 1:2]], axis=0)
        line = jnp.sum(jnp.where(on_diag, tail, 0.0), axis=0, keepdims=True)
        weights = jnp.concatenate([total, under], axis=0) + line
        weights = weights.astype(jnp.bfloat16)[:, :members]
        out_ref[o] = (ens_mean[o] + mm(weights, ens[o])).astype(jnp.bfloat16)

    if oblocks <= 8:
        for o in range(oblocks):
            owner = (2 * o) // picks
            finish(o, owner, o - (owner * picks) // 2)
    else:

        def finish_step(owner, carry):
            for j in range(slots):
                finish(owner * slots + j, owner, j)
            return carry

        lax.fori_loop(0, nm, finish_step, 0)
    for peer in z_peers:
        mix_to(peer).wait_send()


def analysis(send, src, frac, lists, loc, pert, prec, innov, ens):
    ns, nm = lax.axis_size("space"), lax.axis_size("member")
    shard, tile_obs = pert.shape
    members = shard * nm
    oblocks = src.shape[1]
    nc = ns // CORES
    picks = 2 * oblocks // nm
    assert picks * nm == 2 * oblocks and picks <= ROWS16
    assert picks % 2 == 0 or oblocks <= 8
    slots = picks // 2 + picks % 2
    his = tile_obs // LANES
    lobs = lists.shape[1]
    vmem = pl.BlockSpec(memory_space=pltpu.VMEM)
    hbm = pl.BlockSpec(memory_space=pl.ANY)
    dma = pltpu.SemaphoreType.DMA
    bf16, f32 = jnp.bfloat16, jnp.float32
    blocks = lambda n, kind: pltpu.VMEM((n, members, LANES), kind)
    wide = 3 * lobs + 2 * LANES
    big = nc * nm * ns * wide * 2 > 4 * 2**20
    return pl.pallas_call(
        functools.partial(letkf_kernel, ns, nm, picks),
        in_specs=[hbm, hbm, hbm, hbm, hbm, hbm, hbm, hbm, hbm],
        out_specs=vmem,
        out_shape=pltpu.VMEM(ens.shape, bf16),
        scratch_shapes=[
            pltpu.VMEM(lists.shape, lists.dtype),
            pltpu.VMEM(loc.shape, loc.dtype),
            pltpu.VMEM(loc.shape, f32),
            pltpu.VMEM((CORES, nm, shard, tile_obs), bf16),
            pltpu.VMEM((CORES, his, LANES), bf16),
            pltpu.VMEM((CORES, his, LANES), bf16),
            pltpu.VMEM((CORES, his, LANES), f32),
            pltpu.VMEM((CORES, nc * nm, lobs), lists.dtype),
            pltpu.VMEM((CORES, nc * nm, lobs), f32),
            pltpu.VMEM((CORES, nc * nm, wide), bf16),
            pltpu.VMEM((ns, nc * nm, wide), bf16),
            pltpu.VMEM((nc * ROWS16, 3 * lobs), f32),
            pltpu.VMEM((nc * picks, CORES * his, LANES), f32),
            blocks(nc * picks, f32),
            pltpu.VMEM((nc, picks, members // 2, LANES), f32),
            pltpu.VMEM((nc, picks, members // 2, LANES), f32),
            blocks(picks, f32),
            blocks(picks, f32),
            pltpu.VMEM((picks, members, 1), f32),
            pltpu.VMEM((picks, 1, LANES), f32),
            pltpu.VMEM((slots * members // 2, LANES), bf16),
            pltpu.VMEM((nm, slots * members // 2, LANES), bf16),
            pltpu.VMEM(ens.shape, bf16),
            pltpu.VMEM((oblocks, 1, ens.shape[2]), f32),
            pltpu.SMEM(send.shape, send.dtype),
            pltpu.SMEM(src.shape, src.dtype),
            pltpu.SMEM(frac.shape, frac.dtype),
            dma((9,)), dma((nm, PARTS)), dma((nm, PARTS)), dma((nm, PARTS)), dma((nm, PARTS)),
            dma((2,)), dma((2,)), dma((ns,)), dma((ns,)), dma((nc,)), dma((nc,)),
            dma((nm,)), dma((nm,)),
        ],
        compiler_params=pltpu.CompilerParams(
            collective_id=0, has_side_effects=True,
            vmem_limit_bytes=56 * 2**20 if big else None,
        ),
        name="analysis",
    )(send, src, frac, lists, loc, pert, prec, innov, ens)


def shards(
    obs_pert,
    innovation,
    obs_prec,
    obs_lists,
    loc_weight,
    send_rows,
    ocean_src,
    ocean_frac,
    ocean_ens,
):
    result = analysis(
        send_rows[0], ocean_src.T, ocean_frac, obs_lists, loc_weight, obs_pert,
        obs_prec.reshape(-1, LANES), innovation.reshape(-1, LANES),
        ocean_ens.transpose(1, 0, 2),
    )
    return result.transpose(1, 0, 2)


def solution(mesh):
    return jax.shard_map(
        shards,
        mesh=mesh,
        in_specs=(
            P("member", "space"),
            P("space"),
            P("space"),
            P("space", None),
            P("space", None),
            P("space", None, None),
            P("space", None),
            P("space"),
            P(None, "space", "member"),
        ),
        out_specs=P(None, "space", "member"),
        check_vma=False,
    )
```

```python
import functools

import jax
import jax.numpy as jnp
from jax import lax
from jax.experimental import pallas as pl
from jax.experimental.pallas import tpu as pltpu
from jax.sharding import PartitionSpec as P

ITERS = 12
LANES = 128
CORES = 2
ROWS16 = 16
PARTS = 2


def split(value):
    high = value.astype(jnp.bfloat16)
    low = (value - high.astype(jnp.float32)).astype(jnp.bfloat16)
    return high, low


def left_side(value):
    return jnp.concatenate(split(value), axis=1)


def right_side(value):
    pair = left_side(value)
    filler = jnp.zeros((LANES - pair.shape[0], pair.shape[1]), jnp.bfloat16)
    return jnp.concatenate([pair, filler, pair, filler], axis=0)


def halves(product):
    return product[:, :LANES] + product[:, LANES:]


def mm(lhs, rhs):
    return jnp.dot(lhs, rhs, preferred_element_type=jnp.float32)


def xor(value, flip, size):
    result, bit = 0, 1
    while bit < size:
        own = (value // bit) % 2
        result = result + (1 - own if flip & bit else own) * bit
        bit *= 2
    return result


MESH = pl.DeviceIdType.MESH


def remote(src, dst, send_sem, recv_sem, device):
    return pltpu.make_async_remote_copy(
        src_ref=src, dst_ref=dst, send_sem=send_sem, recv_sem=recv_sem,
        device_id=device, device_id_type=MESH,
    )


def letkf_kernel(
    ns, nm, picks,
    send_hbm, src_hbm, frac_hbm, lists_hbm, loc_hbm, pert_ref, prec_ref, innov_ref, ens_hbm, out_ref,
    lists_ref, loc_ref, loc_f32, pert_all, prec_all, innov_all, innov_f32, rows_list, rows_loc,
    message, table, chosen, dense, gram, gram_out, gram_in, root, inverse, pulled, scales, mixed, mixed_in, ens, ens_mean, send_ref, src_ref, frac_ref,
    local_sem, z_send, z_recv, core_send, core_recv, extra_send, extra_recv,
    list_send, list_recv, gram_send, gram_recv, mix_send, mix_recv,
):
    s = lax.axis_index("space")
    m = lax.axis_index("member")
    nc = ns // CORES
    core, chip = s % CORES, s // CORES
    sibling = (s + 1 - 2 * core, m)
    members = pert_ref.shape[0] * nm
    tile_obs = pert_ref.shape[1]
    tile_his = tile_obs // LANES
    cut = tile_his * 6 // 16 * LANES
    bounds = [(0, cut), (cut, tile_obs - cut)]
    group_len = lists_ref.shape[0] // nm
    lobs = lists_ref.shape[1]
    oblocks = out_ref.shape[0]
    slots = mixed.shape[0] // (members // 2)
    z_peers = [xor(m, k, nm) for k in range(1, nm)]
    chips = [xor(chip, k, nc) for k in range(1, nc)]
    s_peers = [lax.rem(s + k, ns) for k in range(1, ns)]

    barrier = pltpu.get_barrier_semaphore()
    for peer in z_peers:
        pl.semaphore_signal(barrier, inc=1, device_id=(s, peer), device_id_type=MESH)
    for peer in s_peers:
        pl.semaphore_signal(barrier, inc=1, device_id=(peer, m), device_id_type=MESH)

    take_lists = pltpu.make_async_copy(lists_hbm, lists_ref, local_sem.at[0])
    take_loc = pltpu.make_async_copy(loc_hbm, loc_ref, local_sem.at[1])
    take_pert = pltpu.make_async_copy(pert_ref, pert_all.at[core, m], local_sem.at[2])
    take_prec = pltpu.make_async_copy(prec_ref, prec_all.at[core], local_sem.at[3])
    take_innov = pltpu.make_async_copy(innov_ref, innov_all.at[core], local_sem.at[4])
    take_ens = pltpu.make_async_copy(ens_hbm, ens, local_sem.at[5])
    take_small = [
        pltpu.make_async_copy(send_hbm, send_ref, local_sem.at[6]),
        pltpu.make_async_copy(src_hbm, src_ref, local_sem.at[7]),
        pltpu.make_async_copy(frac_hbm, frac_ref, local_sem.at[8]),
    ]
    for copy in [take_pert] + take_small + [take_lists, take_loc, take_prec, take_innov, take_ens]:
        copy.start()

    take_pert.wait()
    pl.semaphore_wait(barrier, len(z_peers) + len(s_peers))

    def span(h):
        return pl.ds(*bounds[h])

    def to_z(peer, h):
        return remote(
            pert_all.at[core, m, :, span(h)], pert_all.at[core, m, :, span(h)],
            z_send.at[peer, h], z_recv.at[m, h], (s, peer),
        )

    def from_z(peer, h):
        return remote(
            pert_ref.at[:, span(h)], pert_all.at[core, peer, :, span(h)],
            z_send.at[m, h], z_recv.at[peer, h], (s, peer),
        )

    def across(owner, h, src):
        return remote(
            src, pert_all.at[core, owner, :, span(h)],
            core_send.at[owner, h], core_recv.at[owner, h], sibling,
        )

    def from_across(owner, h):
        there = pert_all.at[1 - core, owner, :, span(h)]
        return remote(there, there, core_send.at[owner, h], core_recv.at[owner, h], sibling)

    for h in range(PARTS):
        for peer in z_peers:
            to_z(peer, h).start()
    extra_out = [
        remote(prec_ref, prec_all.at[core], extra_send.at[0], extra_recv.at[0], sibling),
        remote(innov_ref, innov_all.at[core], extra_send.at[1], extra_recv.at[1], sibling),
    ]
    extra_in = [
        remote(prec_ref, prec_all.at[1 - core], extra_send.at[0], extra_recv.at[0], sibling),
        remote(innov_ref, innov_all.at[1 - core], extra_send.at[1], extra_recv.at[1], sibling),
    ]
    for copy in extra_out:
        copy.start()
    for h in range(PARTS):
        across(m, h, pert_all.at[core, m, :, span(h)]).start()

    for copy in take_small:
        copy.wait()
    take_lists.wait()
    take_loc.wait()
    loc_f32[...] = loc_ref[...].astype(jnp.float32)
    for parity in range(CORES):
        def pick_rows(t, carry):
            for g in range(nm):
                row = send_ref[g, t * CORES + parity] + g * group_len
                rows_list[parity, pl.ds(t * nm + g, 1), :] = lists_ref[pl.ds(row, 1), :]
                rows_loc[parity, pl.ds(t * nm + g, 1), :] = loc_f32[pl.ds(row, 1), :]
            return carry

        lax.fori_loop(0, nc, pick_rows, 0, unroll=nc <= 4)
        spots = rows_list[parity]
        high = lax.shift_right_logical(spots, 7).astype(jnp.float32)
        low = jnp.bitwise_and(spots, LANES - 1).astype(jnp.float32)
        message[parity, :, 0:lobs] = high.astype(jnp.bfloat16)
        message[parity, :, lobs : 2 * lobs] = low.astype(jnp.bfloat16)
        message[parity, :, 2 * lobs : 3 * lobs] = rows_loc[parity].astype(jnp.bfloat16)
    pick_row = lax.broadcasted_iota(jnp.int32, (table.shape[1], LANES), 0)
    tile_of = jnp.zeros((table.shape[1], LANES), jnp.int32)
    group_of = jnp.zeros((table.shape[1], LANES), jnp.int32)
    for p in range(picks):
        q = m * picks + p
        slot = src_ref[q % 2, q // 2]
        tile_of = jnp.where(pick_row == p, slot % ns, tile_of)
        group_of = jnp.where(pick_row == p, slot // ns, group_of)
    for parity in range(CORES):
        message[parity, :, 3 * lobs : 3 * lobs + LANES] = (
            tile_of.astype(jnp.float32).astype(jnp.bfloat16)
        )
        message[parity, :, 3 * lobs + LANES :] = group_of.astype(jnp.float32).astype(jnp.bfloat16)

    def list_to(peer):
        return remote(
            message.at[peer % CORES], table.at[s], list_send.at[peer], list_recv.at[s], (peer, m)
        )

    def list_from(peer):
        return remote(
            message.at[core], table.at[peer], list_send.at[peer], list_recv.at[peer], (peer, m)
        )

    for peer in s_peers:
        list_to(peer).start()
    table[s] = message[core]
    gram[...] = jnp.zeros_like(gram)
    for peer in s_peers:
        list_from(peer).wait_recv()

    deep = nc * ROWS16
    per_tile = table.shape[1]
    tiles_col, rows_col = [], []
    for t in range(nc):
        cut = table[t * CORES + core, 0:ROWS16, 3 * lobs :].astype(jnp.float32)
        tiles_col.append(cut[:, 0:1])
        rows_col.append(cut[:, LANES : LANES + 1] + float(t * nm))
    tiles_col = jnp.concatenate(tiles_col, axis=0).astype(jnp.int32)
    rows_col = jnp.concatenate(rows_col, axis=0).astype(jnp.int32)
    at_row = lax.broadcasted_iota(jnp.int32, (deep, per_tile), 1) == rows_col

    def select(t):
        hot = jnp.where(jnp.logical_and(at_row, tiles_col == t), 1.0, 0.0).astype(jnp.bfloat16)
        return mm(hot, table[t, :, 0 : 3 * lobs])

    if ns <= 8:
        total = select(0)
        for t in range(1, ns):
            total += select(t)
        chosen[...] = total
    else:
        chosen[...] = jnp.zeros_like(chosen)

        def select_step(t, carry):
            chosen[...] += select(t)
            return carry

        lax.fori_loop(0, ns, select_step, 0)
    shift = (tiles_col - 1) * tile_his - chip * (CORES * tile_his)
    spots = chosen[:, 0:lobs] + shift.astype(jnp.float32)
    around = float(ns * tile_his)
    spots = jnp.where(spots < 0.0, spots + around, spots)
    chosen[:, 0:lobs] = jnp.where(spots >= around, spots - around, spots)

    for copy in (take_prec, take_innov):
        copy.wait()
    for copy in extra_in:
        copy.wait_recv()
    innov_f32[...] = innov_all[...].astype(jnp.float32)
    his = CORES * tile_his
    hi_iota = lax.broadcasted_iota(jnp.int32, (his, lobs), 0).astype(jnp.float32)
    lo_iota = lax.broadcasted_iota(jnp.int32, (LANES, lobs), 0).astype(jnp.float32)
    prec = jnp.concatenate([prec_all[i].astype(jnp.float32) for i in range(CORES)], axis=0)
    contract = (((1,), (1,)), ((), ()))

    def spread(t, carry):
        for p in range(picks):
            row = pl.ds(t * ROWS16 + p, 1)
            high, low = chosen[row, 0:lobs], chosen[row, lobs : 2 * lobs]
            taper = chosen[row, 2 * lobs : 3 * lobs]
            hi_hot = jnp.where(hi_iota == high, taper, 0.0).astype(jnp.bfloat16)
            lo_hot = jnp.where(lo_iota == low, 1.0, 0.0).astype(jnp.bfloat16)
            dense[t * picks + p] = prec * lax.dot_general(
                hi_hot, lo_hot, contract, preferred_element_type=jnp.float32
            )
        return carry

    lax.fori_loop(0, nc, spread, 0)

    def take_chunk(tile, h):
        wide = jnp.concatenate(
            [pert_all[tile, i, :, span(h)].astype(jnp.float32) for i in range(nm)], axis=0
        )
        first, count = bounds[h]
        line = jnp.concatenate(
            [
                innov_f32[tile, pl.ds(first // LANES + j, 1), :]
                for j in range(count // LANES)
            ],
            axis=1,
        )
        line = jnp.where(lax.broadcasted_iota(jnp.int32, (ROWS16, count), 0) == 0, line, 0.0)
        return wide, jnp.concatenate([wide, line], axis=0).astype(jnp.bfloat16)

    def add_tile(t, tile, h, wide, cells):
        first = bounds[h][0]
        per = bounds[h][1] // LANES
        for p in range(picks):
            b = t * picks + p
            parts = []
            for j in range(per):
                at = pl.ds(tile * tile_his + first // LANES + j, 1)
                parts.append(wide[:, j * LANES : (j + 1) * LANES] * dense[b, at, :])
            high, low = split(jnp.concatenate(parts, axis=1))
            gram[b, :, : cells.shape[0]] += lax.dot_general(
                high, cells, contract, preferred_element_type=jnp.float32
            ) + lax.dot_general(low, cells, contract, preferred_element_type=jnp.float32)

    def add_part(tile, h):
        wide, cells = take_chunk(tile, h)

        def pick_step(t, carry):
            add_tile(t, tile, h, wide, cells)
            return carry

        lax.fori_loop(0, nc, pick_step, 0, unroll=nc <= 4)

    half = members // 2
    turn = half + 1
    low_cols = lax.broadcasted_iota(jnp.int32, (half, LANES), 1)

    def pack(t):
        for p in range(picks):
            b = t * picks + p
            under = jnp.where(low_cols >= half, gram[b, half:, :], 0.0)
            gram_out[t, p] = gram[b, :half, :] + pltpu.roll(under, turn, 1)

    def arrive(h):
        for peer in z_peers:
            from_z(peer, h).wait_recv()
            across(peer, h, pert_all.at[core, peer, :, span(h)]).start()

    def arrive_across(h):
        for i in range(nm):
            from_across(i, h).wait_recv()

    def gram_to(peer):
        return remote(
            gram_out.at[peer], gram_in.at[chip],
            gram_send.at[peer], gram_recv.at[chip], (peer * CORES + core, m),
        )

    def gram_from(peer):
        return remote(
            gram_out.at[peer], gram_in.at[peer],
            gram_send.at[peer], gram_recv.at[peer], (peer * CORES + core, m),
        )

    for h in range(PARTS):
        arrive(h)
        add_part(core, h)
        arrive_across(h)
        if h + 1 < PARTS or nc > 4:
            add_part(1 - core, h)

    if nc <= 4:
        wide, cells = take_chunk(1 - core, PARTS - 1)
        for t in chips[::-1] + [chip]:
            add_tile(t, 1 - core, PARTS - 1, wide, cells)
            pack(t)
            if t is not chip:
                gram_to(t).start()
    else:

        def pack_step(t, carry):
            pack(t)
            return carry

        lax.fori_loop(0, nc, pack_step, 0)
        for peer in reversed(chips):
            gram_to(peer).start()

    take_ens.wait()

    def center(o, carry):
        wide = ens[o].astype(jnp.float32)
        mean = jnp.sum(wide, axis=0, keepdims=True) * (1.0 / members)
        ens_mean[o] = mean
        ens[o] = (wide - mean).astype(jnp.bfloat16)
        return carry

    lax.fori_loop(0, oblocks, center, 0)

    rows = lax.broadcasted_iota(jnp.int32, (members, LANES), 0)
    cols = lax.broadcasted_iota(jnp.int32, (members, LANES), 1)
    on_diag = rows == cols
    half3 = jnp.where(on_diag, 1.5, 0.0)

    for peer in chips:
        gram_from(peer).wait_recv()
    filler = jnp.zeros((LANES - half, LANES), jnp.float32)
    for p in range(picks):
        top = gram_out[chip, p]
        for peer in chips:
            top += gram_in[peer, p]
        under = pltpu.roll(top, LANES - turn, 1)
        flipped = jnp.concatenate([top, filler], axis=0).T[half : 2 * half]
        both = jnp.concatenate([top, jnp.where(low_cols < half, flipped, under)], axis=0)
        pulled[p] = jnp.sum(jnp.where(cols == members, both, 0.0), axis=1, keepdims=True)
        matrix = jnp.where(cols < members, both, 0.0) + jnp.where(on_diag, members - 1.0, 0.0)
        scale = jnp.sum(
            jnp.sum(jnp.where(on_diag, matrix, 0.0), axis=1, keepdims=True), axis=0, keepdims=True
        )
        scales[p] = jnp.broadcast_to(scale, (1, LANES))
        start = matrix / scale
        correction = half3 - 0.5 * start
        root[p] = halves(mm(left_side(start), right_side(correction)))
        inverse[p] = correction

    def newton(step, carry, last=False):
        corrections, pairs = [], []
        space = jnp.zeros((LANES - members, 2 * LANES), jnp.bfloat16)
        for p in range(picks):
            r, z = left_side(root[p]), left_side(inverse[p])
            rhs = jnp.concatenate([r, space, r, space], axis=0)
            corrections.append(half3 - 0.5 * halves(mm(z, rhs)))
            pairs.append(z if last else jnp.concatenate([r, z], axis=0))
        for p in range(picks):
            both = halves(mm(pairs[p], right_side(corrections[p])))
            if not last:
                root[p] = both[:members]
            inverse[p] = both[-members:]
        return carry

    lax.fori_loop(0, ITERS - 2, newton, 0, unroll=picks <= 4)
    newton(ITERS - 2, 0, last=True)

    sums = [jnp.zeros((members, LANES), jnp.float32) for _ in range(slots)]
    means = [jnp.zeros((members, 1), jnp.float32) for _ in range(slots)]
    base = (m * picks) // 2
    for p in range(picks):
        z = inverse[p]
        scale = scales[p]
        half_way = jnp.sum(z * pulled[p], axis=0, keepdims=True)
        mean_weight = jnp.sum(z * half_way, axis=1, keepdims=True) / scale[:, :1]
        trans = jnp.sqrt((members - 1.0) / scale) * z
        q = m * picks + p
        o = q // 2
        frac = frac_ref[o]
        weight = jnp.where(q % 2 == 0, 1.0 - frac, frac)
        for j in range(max(0, p // 2), min(slots, p // 2 + 2)):
            share = jnp.where(o - base == j, weight, 0.0)
            sums[j] += share * trans
            means[j] += share * mean_weight
    for j in range(slots):
        under = jnp.where(low_cols < half, 0.0, jnp.where(low_cols < members, sums[j][half:], 0.0))
        packed = sums[j][:half] + pltpu.roll(under, half, 1)
        high = means[j].astype(jnp.bfloat16).astype(jnp.float32)
        tails = (high, means[j] - high)
        for k in range(4):
            tail = tails[k // 2][(k % 2) * half : (k % 2 + 1) * half]
            packed = jnp.where(low_cols == members + half + k, tail, packed)
        mixed[j * half : (j + 1) * half, :] = packed.astype(jnp.bfloat16)

    def mix_to(peer):
        return remote(mixed, mixed_in.at[m], mix_send.at[peer], mix_recv.at[m], (s, peer))

    def mix_from(peer):
        return remote(mixed, mixed_in.at[peer], mix_send.at[peer], mix_recv.at[peer], (s, peer))

    for peer in z_peers:
        mix_to(peer).start()
    mixed_in[m] = mixed[...]
    for peer in chips:
        gram_to(peer).wait_send()
    for peer in s_peers:
        list_to(peer).wait_send()
    for copy in extra_out:
        copy.wait_send()
    for h in range(PARTS):
        for peer in z_peers:
            to_z(peer, h).wait_send()
            across(peer, h, pert_all.at[core, peer, :, span(h)]).wait_send()
        across(m, h, pert_all.at[core, m, :, span(h)]).wait_send()
    def finish(pair, first):
        o = pair * picks + first
        total = None
        for k in range(2):
            j = first - (picks * k) // 2
            if 0 <= j < slots:
                term = mixed_in[2 * pair + k, j * half : (j + 1) * half].astype(jnp.float32)
                total = term if total is None else total + term
        flipped = jnp.concatenate([total, filler], axis=0).T[half : 2 * half]
        under = jnp.where(low_cols < half, flipped, pltpu.roll(total, LANES - half, 1))
        at = members + half
        tail = total[:, at : at + 2] + total[:, at + 2 : at + 4]
        tail = jnp.concatenate([tail[:, 0:1], tail[:, 1:2]], axis=0)
        line = jnp.sum(jnp.where(on_diag, tail, 0.0), axis=0, keepdims=True)
        weights = jnp.concatenate([total, under], axis=0) + line
        weights = weights.astype(jnp.bfloat16)[:, :members]
        out_ref[o] = (ens_mean[o] + mm(weights, ens[o])).astype(jnp.bfloat16)

    for k in range(0, nm, 2):
        for peer in z_peers[max(k - 1, 0) : k + 1]:
            mix_from(peer).wait_recv()
        for first in range(picks):
            finish(xor(m, k, nm) // 2, first)
    for peer in z_peers:
        mix_to(peer).wait_send()


def analysis(send, src, frac, lists, loc, pert, prec, innov, ens):
    ns, nm = lax.axis_size("space"), lax.axis_size("member")
    shard, tile_obs = pert.shape
    members = shard * nm
    oblocks = src.shape[1]
    nc = ns // CORES
    picks = 2 * oblocks // nm
    assert picks * nm == 2 * oblocks and picks <= ROWS16
    assert nm % 2 == 0
    slots = picks // 2 + picks % 2
    his = tile_obs // LANES
    lobs = lists.shape[1]
    vmem = pl.BlockSpec(memory_space=pltpu.VMEM)
    hbm = pl.BlockSpec(memory_space=pl.ANY)
    dma = pltpu.SemaphoreType.DMA
    bf16, f32 = jnp.bfloat16, jnp.float32
    blocks = lambda n, kind: pltpu.VMEM((n, members, LANES), kind)
    wide = 3 * lobs + 2 * LANES
    big = nc * nm * ns * wide * 2 > 4 * 2**20
    return pl.pallas_call(
        functools.partial(letkf_kernel, ns, nm, picks),
        in_specs=[hbm, hbm, hbm, hbm, hbm, hbm, hbm, hbm, hbm],
        out_specs=vmem,
        out_shape=pltpu.VMEM(ens.shape, bf16),
        scratch_shapes=[
            pltpu.VMEM(lists.shape, lists.dtype),
            pltpu.VMEM(loc.shape, loc.dtype),
            pltpu.VMEM(loc.shape, f32),
            pltpu.VMEM((CORES, nm, shard, tile_obs), bf16),
            pltpu.VMEM((CORES, his, LANES), bf16),
            pltpu.VMEM((CORES, his, LANES), bf16),
            pltpu.VMEM((CORES, his, LANES), f32),
            pltpu.VMEM((CORES, nc * nm, lobs), lists.dtype),
            pltpu.VMEM((CORES, nc * nm, lobs), f32),
            pltpu.VMEM((CORES, nc * nm, wide), bf16),
            pltpu.VMEM((ns, nc * nm, wide), bf16),
            pltpu.VMEM((nc * ROWS16, 3 * lobs), f32),
            pltpu.VMEM((nc * picks, CORES * his, LANES), f32),
            blocks(nc * picks, f32),
            pltpu.VMEM((nc, picks, members // 2, LANES), f32),
            pltpu.VMEM((nc, picks, members // 2, LANES), f32),
            blocks(picks, f32),
            blocks(picks, f32),
            pltpu.VMEM((picks, members, 1), f32),
            pltpu.VMEM((picks, 1, LANES), f32),
            pltpu.VMEM((slots * members // 2, LANES), bf16),
            pltpu.VMEM((nm, slots * members // 2, LANES), bf16),
            pltpu.VMEM(ens.shape, bf16),
            pltpu.VMEM((oblocks, 1, ens.shape[2]), f32),
            pltpu.SMEM(send.shape, send.dtype),
            pltpu.SMEM(src.shape, src.dtype),
            pltpu.SMEM(frac.shape, frac.dtype),
            dma((9,)), dma((nm, PARTS)), dma((nm, PARTS)), dma((nm, PARTS)), dma((nm, PARTS)),
            dma((2,)), dma((2,)), dma((ns,)), dma((ns,)), dma((nc,)), dma((nc,)),
            dma((nm,)), dma((nm,)),
        ],
        compiler_params=pltpu.CompilerParams(
            collective_id=0, has_side_effects=True,
            vmem_limit_bytes=56 * 2**20 if big else None,
        ),
        name="analysis",
    )(send, src, frac, lists, loc, pert, prec, innov, ens)


def shards(
    obs_pert,
    innovation,
    obs_prec,
    obs_lists,
    loc_weight,
    send_rows,
    ocean_src,
    ocean_frac,
    ocean_ens,
):
    result = analysis(
        send_rows[0], ocean_src.T, ocean_frac, obs_lists, loc_weight, obs_pert,
        obs_prec.reshape(-1, LANES), innovation.reshape(-1, LANES),
        ocean_ens.transpose(1, 0, 2),
    )
    return result.transpose(1, 0, 2)


def solution(mesh):
    return jax.shard_map(
        shards,
        mesh=mesh,
        in_specs=(
            P("member", "space"),
            P("space"),
            P("space"),
            P("space", None),
            P("space", None),
            P("space", None, None),
            P("space", None),
            P("space"),
            P(None, "space", "member"),
        ),
        out_specs=P(None, "space", "member"),
        check_vma=False,
    )
```

```python
import functools

import jax
import jax.numpy as jnp
from jax import lax
from jax.experimental import pallas as pl
from jax.experimental.pallas import tpu as pltpu
from jax.sharding import PartitionSpec as P

ITERS = 12
LANES = 128
CORES = 2
ROWS16 = 16
PARTS = 2


def split(value):
    high = value.astype(jnp.bfloat16)
    low = (value - high.astype(jnp.float32)).astype(jnp.bfloat16)
    return high, low


def left_side(value):
    return jnp.concatenate(split(value), axis=1)


def right_side(value):
    pair = left_side(value)
    filler = jnp.zeros((LANES - pair.shape[0], pair.shape[1]), jnp.bfloat16)
    return jnp.concatenate([pair, filler, pair, filler], axis=0)


def halves(product):
    return product[:, :LANES] + product[:, LANES:]


def mm(lhs, rhs):
    return jnp.dot(lhs, rhs, preferred_element_type=jnp.float32)


def xor(value, flip, size):
    result, bit = 0, 1
    while bit < size:
        own = (value // bit) % 2
        result = result + (1 - own if flip & bit else own) * bit
        bit *= 2
    return result


MESH = pl.DeviceIdType.MESH


def remote(src, dst, send_sem, recv_sem, device):
    return pltpu.make_async_remote_copy(
        src_ref=src, dst_ref=dst, send_sem=send_sem, recv_sem=recv_sem,
        device_id=device, device_id_type=MESH,
    )


def letkf_kernel(
    ns, nm, picks,
    send_hbm, src_hbm, frac_hbm, lists_hbm, loc_hbm, pert_ref, prec_ref, innov_ref, ens_hbm, out_ref,
    lists_ref, loc_ref, loc_f32, pert_all, prec_all, innov_all, innov_f32, rows_list, rows_loc,
    message, table, chosen, dense, gram, gram_out, gram_in, root, inverse, pulled, scales, mixed, mixed_in, ens, ens_mean, send_ref, src_ref, frac_ref,
    local_sem, z_send, z_recv, core_send, core_recv, extra_send, extra_recv,
    list_send, list_recv, gram_send, gram_recv, mix_send, mix_recv,
):
    s = lax.axis_index("space")
    m = lax.axis_index("member")
    nc = ns // CORES
    core, chip = s % CORES, s // CORES
    sibling = (s + 1 - 2 * core, m)
    members = pert_ref.shape[0] * nm
    tile_obs = pert_ref.shape[1]
    tile_his = tile_obs // LANES
    cut = tile_his * 6 // 16 * LANES
    bounds = [(0, cut), (cut, tile_obs - cut)]
    group_len = lists_ref.shape[0] // nm
    lobs = lists_ref.shape[1]
    oblocks = out_ref.shape[0]
    slots = mixed.shape[0] // (members // 2)
    z_peers = [xor(m, k, nm) for k in range(1, nm)]
    chips = [xor(chip, k, nc) for k in range(1, nc)]
    s_peers = [lax.rem(s + k, ns) for k in range(1, ns)]

    barrier = pltpu.get_barrier_semaphore()
    for peer in z_peers:
        pl.semaphore_signal(barrier, inc=1, device_id=(s, peer), device_id_type=MESH)
    for peer in s_peers:
        pl.semaphore_signal(barrier, inc=1, device_id=(peer, m), device_id_type=MESH)

    take_lists = pltpu.make_async_copy(lists_hbm, lists_ref, local_sem.at[0])
    take_loc = pltpu.make_async_copy(loc_hbm, loc_ref, local_sem.at[1])
    take_pert = pltpu.make_async_copy(pert_ref, pert_all.at[core, m], local_sem.at[2])
    take_prec = pltpu.make_async_copy(prec_ref, prec_all.at[core], local_sem.at[3])
    take_innov = pltpu.make_async_copy(innov_ref, innov_all.at[core], local_sem.at[4])
    take_ens = pltpu.make_async_copy(ens_hbm, ens, local_sem.at[5])
    take_small = [
        pltpu.make_async_copy(send_hbm, send_ref, local_sem.at[6]),
        pltpu.make_async_copy(src_hbm, src_ref, local_sem.at[7]),
        pltpu.make_async_copy(frac_hbm, frac_ref, local_sem.at[8]),
    ]
    for copy in [take_pert] + take_small + [take_lists, take_loc, take_prec, take_innov, take_ens]:
        copy.start()

    for copy in take_small:
        copy.wait()
    take_lists.wait()
    take_loc.wait()
    loc_f32[...] = loc_ref[...].astype(jnp.float32)
    for parity in range(CORES):
        def pick_rows(t, carry):
            for g in range(nm):
                row = send_ref[g, t * CORES + parity] + g * group_len
                rows_list[parity, pl.ds(t * nm + g, 1), :] = lists_ref[pl.ds(row, 1), :]
                rows_loc[parity, pl.ds(t * nm + g, 1), :] = loc_f32[pl.ds(row, 1), :]
            return carry

        lax.fori_loop(0, nc, pick_rows, 0, unroll=nc <= 4)
        spots = rows_list[parity]
        high = lax.shift_right_logical(spots, 7).astype(jnp.float32)
        low = jnp.bitwise_and(spots, LANES - 1).astype(jnp.float32)
        message[parity, :, 0:lobs] = high.astype(jnp.bfloat16)
        message[parity, :, lobs : 2 * lobs] = low.astype(jnp.bfloat16)
        message[parity, :, 2 * lobs : 3 * lobs] = rows_loc[parity].astype(jnp.bfloat16)
    pick_row = lax.broadcasted_iota(jnp.int32, (table.shape[1], LANES), 0)
    tile_of = jnp.zeros((table.shape[1], LANES), jnp.int32)
    group_of = jnp.zeros((table.shape[1], LANES), jnp.int32)
    for p in range(picks):
        q = m * picks + p
        slot = src_ref[q % 2, q // 2]
        tile_of = jnp.where(pick_row == p, slot % ns, tile_of)
        group_of = jnp.where(pick_row == p, slot // ns, group_of)
    for parity in range(CORES):
        message[parity, :, 3 * lobs : 3 * lobs + LANES] = (
            tile_of.astype(jnp.float32).astype(jnp.bfloat16)
        )
        message[parity, :, 3 * lobs + LANES :] = group_of.astype(jnp.float32).astype(jnp.bfloat16)

    take_pert.wait()
    pl.semaphore_wait(barrier, len(z_peers) + len(s_peers))

    def span(h):
        return pl.ds(*bounds[h])

    def to_z(peer, h):
        return remote(
            pert_all.at[core, m, :, span(h)], pert_all.at[core, m, :, span(h)],
            z_send.at[peer, h], z_recv.at[m, h], (s, peer),
        )

    def from_z(peer, h):
        return remote(
            pert_ref.at[:, span(h)], pert_all.at[core, peer, :, span(h)],
            z_send.at[m, h], z_recv.at[peer, h], (s, peer),
        )

    def across(owner, h, src):
        return remote(
            src, pert_all.at[core, owner, :, span(h)],
            core_send.at[owner, h], core_recv.at[owner, h], sibling,
        )

    def from_across(owner, h):
        there = pert_all.at[1 - core, owner, :, span(h)]
        return remote(there, there, core_send.at[owner, h], core_recv.at[owner, h], sibling)

    for h in range(PARTS):
        for peer in z_peers:
            to_z(peer, h).start()
    extra_out = [
        remote(prec_ref, prec_all.at[core], extra_send.at[0], extra_recv.at[0], sibling),
        remote(innov_ref, innov_all.at[core], extra_send.at[1], extra_recv.at[1], sibling),
    ]
    extra_in = [
        remote(prec_ref, prec_all.at[1 - core], extra_send.at[0], extra_recv.at[0], sibling),
        remote(innov_ref, innov_all.at[1 - core], extra_send.at[1], extra_recv.at[1], sibling),
    ]
    for copy in extra_out:
        copy.start()
    for h in range(PARTS):
        across(m, h, pert_all.at[core, m, :, span(h)]).start()

    def list_to(peer):
        return remote(
            message.at[peer % CORES], table.at[s], list_send.at[peer], list_recv.at[s], (peer, m)
        )

    def list_from(peer):
        return remote(
            message.at[core], table.at[peer], list_send.at[peer], list_recv.at[peer], (peer, m)
        )

    for peer in s_peers:
        list_to(peer).start()
    table[s] = message[core]
    gram[...] = jnp.zeros_like(gram)
    for peer in s_peers:
        list_from(peer).wait_recv()

    deep = nc * ROWS16
    per_tile = table.shape[1]
    tiles_col, rows_col = [], []
    for t in range(nc):
        cut = table[t * CORES + core, 0:ROWS16, 3 * lobs :].astype(jnp.float32)
        tiles_col.append(cut[:, 0:1])
        rows_col.append(cut[:, LANES : LANES + 1] + float(t * nm))
    tiles_col = jnp.concatenate(tiles_col, axis=0).astype(jnp.int32)
    rows_col = jnp.concatenate(rows_col, axis=0).astype(jnp.int32)
    at_row = lax.broadcasted_iota(jnp.int32, (deep, per_tile), 1) == rows_col

    def select(t):
        hot = jnp.where(jnp.logical_and(at_row, tiles_col == t), 1.0, 0.0).astype(jnp.bfloat16)
        return mm(hot, table[t, :, 0 : 3 * lobs])

    if ns <= 8:
        total = select(0)
        for t in range(1, ns):
            total += select(t)
        chosen[...] = total
    else:
        chosen[...] = jnp.zeros_like(chosen)

        def select_step(t, carry):
            chosen[...] += select(t)
            return carry

        lax.fori_loop(0, ns, select_step, 0)
    shift = (tiles_col - 1) * tile_his - chip * (CORES * tile_his)
    spots = chosen[:, 0:lobs] + shift.astype(jnp.float32)
    around = float(ns * tile_his)
    spots = jnp.where(spots < 0.0, spots + around, spots)
    chosen[:, 0:lobs] = jnp.where(spots >= around, spots - around, spots)

    for copy in (take_prec, take_innov):
        copy.wait()
    for copy in extra_in:
        copy.wait_recv()
    innov_f32[...] = innov_all[...].astype(jnp.float32)
    his = CORES * tile_his
    hi_iota = lax.broadcasted_iota(jnp.int32, (his, lobs), 0).astype(jnp.float32)
    lo_iota = lax.broadcasted_iota(jnp.int32, (LANES, lobs), 0).astype(jnp.float32)
    prec = jnp.concatenate([prec_all[i].astype(jnp.float32) for i in range(CORES)], axis=0)
    contract = (((1,), (1,)), ((), ()))

    def spread(t, carry):
        for p in range(picks):
            row = pl.ds(t * ROWS16 + p, 1)
            high, low = chosen[row, 0:lobs], chosen[row, lobs : 2 * lobs]
            taper = chosen[row, 2 * lobs : 3 * lobs]
            hi_hot = jnp.where(hi_iota == high, taper, 0.0).astype(jnp.bfloat16)
            lo_hot = jnp.where(lo_iota == low, 1.0, 0.0).astype(jnp.bfloat16)
            dense[t * picks + p] = prec * lax.dot_general(
                hi_hot, lo_hot, contract, preferred_element_type=jnp.float32
            )
        return carry

    lax.fori_loop(0, nc, spread, 0)

    def take_chunk(tile, h):
        wide = jnp.concatenate(
            [pert_all[tile, i, :, span(h)].astype(jnp.float32) for i in range(nm)], axis=0
        )
        first, count = bounds[h]
        line = jnp.concatenate(
            [
                innov_f32[tile, pl.ds(first // LANES + j, 1), :]
                for j in range(count // LANES)
            ],
            axis=1,
        )
        line = jnp.where(lax.broadcasted_iota(jnp.int32, (ROWS16, count), 0) == 0, line, 0.0)
        return wide, jnp.concatenate([wide, line], axis=0).astype(jnp.bfloat16)

    def add_tile(t, tile, h, wide, cells):
        first = bounds[h][0]
        per = bounds[h][1] // LANES
        for p in range(picks):
            b = t * picks + p
            parts = []
            for j in range(per):
                at = pl.ds(tile * tile_his + first // LANES + j, 1)
                parts.append(wide[:, j * LANES : (j + 1) * LANES] * dense[b, at, :])
            high, low = split(jnp.concatenate(parts, axis=1))
            gram[b, :, : cells.shape[0]] += lax.dot_general(
                high, cells, contract, preferred_element_type=jnp.float32
            ) + lax.dot_general(low, cells, contract, preferred_element_type=jnp.float32)

    def add_part(tile, h):
        wide, cells = take_chunk(tile, h)

        def pick_step(t, carry):
            add_tile(t, tile, h, wide, cells)
            return carry

        lax.fori_loop(0, nc, pick_step, 0, unroll=nc <= 4)

    half = members // 2
    turn = half + 1
    low_cols = lax.broadcasted_iota(jnp.int32, (half, LANES), 1)

    def pack(t):
        for p in range(picks):
            b = t * picks + p
            under = jnp.where(low_cols >= half, gram[b, half:, :], 0.0)
            gram_out[t, p] = gram[b, :half, :] + pltpu.roll(under, turn, 1)

    def arrive(h):
        for peer in z_peers:
            from_z(peer, h).wait_recv()
            across(peer, h, pert_all.at[core, peer, :, span(h)]).start()

    def arrive_across(h):
        for i in range(nm):
            from_across(i, h).wait_recv()

    def gram_to(peer):
        return remote(
            gram_out.at[peer], gram_in.at[chip],
            gram_send.at[peer], gram_recv.at[chip], (peer * CORES + core, m),
        )

    def gram_from(peer):
        return remote(
            gram_out.at[peer], gram_in.at[peer],
            gram_send.at[peer], gram_recv.at[peer], (peer * CORES + core, m),
        )

    for h in range(PARTS):
        arrive(h)
        add_part(core, h)
        arrive_across(h)
        if h + 1 < PARTS or nc > 4:
            add_part(1 - core, h)

    if nc <= 4:
        wide, cells = take_chunk(1 - core, PARTS - 1)
        for t in chips[::-1] + [chip]:
            add_tile(t, 1 - core, PARTS - 1, wide, cells)
            pack(t)
            if t is not chip:
                gram_to(t).start()
    else:

        def pack_step(t, carry):
            pack(t)
            return carry

        lax.fori_loop(0, nc, pack_step, 0)
        for peer in reversed(chips):
            gram_to(peer).start()

    take_ens.wait()

    def center(o, carry):
        wide = ens[o].astype(jnp.float32)
        mean = jnp.sum(wide, axis=0, keepdims=True) * (1.0 / members)
        ens_mean[o] = mean
        ens[o] = (wide - mean).astype(jnp.bfloat16)
        return carry

    lax.fori_loop(0, oblocks, center, 0)

    rows = lax.broadcasted_iota(jnp.int32, (members, LANES), 0)
    cols = lax.broadcasted_iota(jnp.int32, (members, LANES), 1)
    on_diag = rows == cols
    half3 = jnp.where(on_diag, 1.5, 0.0)

    for peer in chips:
        gram_from(peer).wait_recv()
    filler = jnp.zeros((LANES - half, LANES), jnp.float32)
    for p in range(picks):
        top = gram_out[chip, p]
        for peer in chips:
            top += gram_in[peer, p]
        under = pltpu.roll(top, LANES - turn, 1)
        flipped = jnp.concatenate([top, filler], axis=0).T[half : 2 * half]
        both = jnp.concatenate([top, jnp.where(low_cols < half, flipped, under)], axis=0)
        pulled[p] = jnp.sum(jnp.where(cols == members, both, 0.0), axis=1, keepdims=True)
        matrix = jnp.where(cols < members, both, 0.0) + jnp.where(on_diag, members - 1.0, 0.0)
        scale = jnp.sum(
            jnp.sum(jnp.where(on_diag, matrix, 0.0), axis=1, keepdims=True), axis=0, keepdims=True
        )
        scales[p] = jnp.broadcast_to(scale, (1, LANES))
        start = matrix / scale
        correction = half3 - 0.5 * start
        root[p] = halves(mm(left_side(start), right_side(correction)))
        inverse[p] = correction

    def newton(step, carry, last=False):
        corrections, pairs = [], []
        space = jnp.zeros((LANES - members, 2 * LANES), jnp.bfloat16)
        for p in range(picks):
            r, z = left_side(root[p]), left_side(inverse[p])
            rhs = jnp.concatenate([r, space, r, space], axis=0)
            corrections.append(half3 - 0.5 * halves(mm(z, rhs)))
            pairs.append(z if last else jnp.concatenate([r, z], axis=0))
        for p in range(picks):
            both = halves(mm(pairs[p], right_side(corrections[p])))
            if not last:
                root[p] = both[:members]
            inverse[p] = both[-members:]
        return carry

    lax.fori_loop(0, ITERS - 2, newton, 0, unroll=picks <= 4)
    newton(ITERS - 2, 0, last=True)

    sums = [jnp.zeros((members, LANES), jnp.float32) for _ in range(slots)]
    means = [jnp.zeros((members, 1), jnp.float32) for _ in range(slots)]
    base = (m * picks) // 2
    for p in range(picks):
        z = inverse[p]
        scale = scales[p]
        half_way = jnp.sum(z * pulled[p], axis=0, keepdims=True)
        mean_weight = jnp.sum(z * half_way, axis=1, keepdims=True) / scale[:, :1]
        trans = jnp.sqrt((members - 1.0) / scale) * z
        q = m * picks + p
        o = q // 2
        frac = frac_ref[o]
        weight = jnp.where(q % 2 == 0, 1.0 - frac, frac)
        for j in range(max(0, p // 2), min(slots, p // 2 + 2)):
            share = jnp.where(o - base == j, weight, 0.0)
            sums[j] += share * trans
            means[j] += share * mean_weight
    for j in range(slots):
        under = jnp.where(low_cols < half, 0.0, jnp.where(low_cols < members, sums[j][half:], 0.0))
        packed = sums[j][:half] + pltpu.roll(under, half, 1)
        high = means[j].astype(jnp.bfloat16).astype(jnp.float32)
        tails = (high, means[j] - high)
        for k in range(4):
            tail = tails[k // 2][(k % 2) * half : (k % 2 + 1) * half]
            packed = jnp.where(low_cols == members + half + k, tail, packed)
        mixed[j * half : (j + 1) * half, :] = packed.astype(jnp.bfloat16)

    def mix_to(peer):
        return remote(mixed, mixed_in.at[m], mix_send.at[peer], mix_recv.at[m], (s, peer))

    def mix_from(peer):
        return remote(mixed, mixed_in.at[peer], mix_send.at[peer], mix_recv.at[peer], (s, peer))

    for peer in z_peers:
        mix_to(peer).start()
    mixed_in[m] = mixed[...]
    for peer in chips:
        gram_to(peer).wait_send()
    for peer in s_peers:
        list_to(peer).wait_send()
    for copy in extra_out:
        copy.wait_send()
    for h in range(PARTS):
        for peer in z_peers:
            to_z(peer, h).wait_send()
            across(peer, h, pert_all.at[core, peer, :, span(h)]).wait_send()
        across(m, h, pert_all.at[core, m, :, span(h)]).wait_send()
    def finish(pair, first):
        o = pair * picks + first
        total = None
        for k in range(2):
            j = first - (picks * k) // 2
            if 0 <= j < slots:
                term = mixed_in[2 * pair + k, j * half : (j + 1) * half].astype(jnp.float32)
                total = term if total is None else total + term
        flipped = jnp.concatenate([total, filler], axis=0).T[half : 2 * half]
        under = jnp.where(low_cols < half, flipped, pltpu.roll(total, LANES - half, 1))
        at = members + half
        tail = total[:, at : at + 2] + total[:, at + 2 : at + 4]
        tail = jnp.concatenate([tail[:, 0:1], tail[:, 1:2]], axis=0)
        line = jnp.sum(jnp.where(on_diag, tail, 0.0), axis=0, keepdims=True)
        weights = jnp.concatenate([total, under], axis=0) + line
        weights = weights.astype(jnp.bfloat16)[:, :members]
        out_ref[o] = (ens_mean[o] + mm(weights, ens[o])).astype(jnp.bfloat16)

    for k in range(0, nm, 2):
        for peer in z_peers[max(k - 1, 0) : k + 1]:
            mix_from(peer).wait_recv()
        for first in range(picks):
            finish(xor(m, k, nm) // 2, first)
    for peer in z_peers:
        mix_to(peer).wait_send()


def analysis(send, src, frac, lists, loc, pert, prec, innov, ens):
    ns, nm = lax.axis_size("space"), lax.axis_size("member")
    shard, tile_obs = pert.shape
    members = shard * nm
    oblocks = src.shape[1]
    nc = ns // CORES
    picks = 2 * oblocks // nm
    assert picks * nm == 2 * oblocks and picks <= ROWS16
    assert nm % 2 == 0
    slots = picks // 2 + picks % 2
    his = tile_obs // LANES
    lobs = lists.shape[1]
    vmem = pl.BlockSpec(memory_space=pltpu.VMEM)
    hbm = pl.BlockSpec(memory_space=pl.ANY)
    dma = pltpu.SemaphoreType.DMA
    bf16, f32 = jnp.bfloat16, jnp.float32
    blocks = lambda n, kind: pltpu.VMEM((n, members, LANES), kind)
    wide = 3 * lobs + 2 * LANES
    big = nc * nm * ns * wide * 2 > 4 * 2**20
    return pl.pallas_call(
        functools.partial(letkf_kernel, ns, nm, picks),
        in_specs=[hbm, hbm, hbm, hbm, hbm, hbm, hbm, hbm, hbm],
        out_specs=vmem,
        out_shape=pltpu.VMEM(ens.shape, bf16),
        scratch_shapes=[
            pltpu.VMEM(lists.shape, lists.dtype),
            pltpu.VMEM(loc.shape, loc.dtype),
            pltpu.VMEM(loc.shape, f32),
            pltpu.VMEM((CORES, nm, shard, tile_obs), bf16),
            pltpu.VMEM((CORES, his, LANES), bf16),
            pltpu.VMEM((CORES, his, LANES), bf16),
            pltpu.VMEM((CORES, his, LANES), f32),
            pltpu.VMEM((CORES, nc * nm, lobs), lists.dtype),
            pltpu.VMEM((CORES, nc * nm, lobs), f32),
            pltpu.VMEM((CORES, nc * nm, wide), bf16),
            pltpu.VMEM((ns, nc * nm, wide), bf16),
            pltpu.VMEM((nc * ROWS16, 3 * lobs), f32),
            pltpu.VMEM((nc * picks, CORES * his, LANES), f32),
            blocks(nc * picks, f32),
            pltpu.VMEM((nc, picks, members // 2, LANES), f32),
            pltpu.VMEM((nc, picks, members // 2, LANES), f32),
            blocks(picks, f32),
            blocks(picks, f32),
            pltpu.VMEM((picks, members, 1), f32),
            pltpu.VMEM((picks, 1, LANES), f32),
            pltpu.VMEM((slots * members // 2, LANES), bf16),
            pltpu.VMEM((nm, slots * members // 2, LANES), bf16),
            pltpu.VMEM(ens.shape, bf16),
            pltpu.VMEM((oblocks, 1, ens.shape[2]), f32),
            pltpu.SMEM(send.shape, send.dtype),
            pltpu.SMEM(src.shape, src.dtype),
            pltpu.SMEM(frac.shape, frac.dtype),
            dma((9,)), dma((nm, PARTS)), dma((nm, PARTS)), dma((nm, PARTS)), dma((nm, PARTS)),
            dma((2,)), dma((2,)), dma((ns,)), dma((ns,)), dma((nc,)), dma((nc,)),
            dma((nm,)), dma((nm,)),
        ],
        compiler_params=pltpu.CompilerParams(
            collective_id=0, has_side_effects=True,
            vmem_limit_bytes=56 * 2**20 if big else None,
        ),
        name="analysis",
    )(send, src, frac, lists, loc, pert, prec, innov, ens)


def shards(
    obs_pert,
    innovation,
    obs_prec,
    obs_lists,
    loc_weight,
    send_rows,
    ocean_src,
    ocean_frac,
    ocean_ens,
):
    result = analysis(
        send_rows[0], ocean_src.T, ocean_frac, obs_lists, loc_weight, obs_pert,
        obs_prec.reshape(-1, LANES), innovation.reshape(-1, LANES),
        ocean_ens.transpose(1, 0, 2),
    )
    return result.transpose(1, 0, 2)


def solution(mesh):
    return jax.shard_map(
        shards,
        mesh=mesh,
        in_specs=(
            P("member", "space"),
            P("space"),
            P("space"),
            P("space", None),
            P("space", None),
            P("space", None, None),
            P("space", None),
            P("space"),
            P(None, "space", "member"),
        ),
        out_specs=P(None, "space", "member"),
        check_vma=False,
    )
```
